256 devices in a mesh: dp: 2 (over y_hi), ctx: 64 (over x, z, core), head: 2 (over y_lo).
Axes of the slice: x: 4, y: 4 (y_hi: 2, y_lo: 2; y = y_hi * 2 + y_lo), z: 8, core: 2. Of those that a mesh axis runs over, the one named last changes fastest.
Arguments:
- queries: bfloat16 [8192, 4, 1024], P('ctx', ('dp', 'head')), may hold values from -5 to 5
- keys: bfloat16 [8192, 4, 128], P(('ctx', 'head', 'dp')), may hold values from -5 to 5
- values: bfloat16 [8192, 4, 128], P(('ctx', 'head', 'dp')), may hold values from -6 to 6
- outputs: bfloat16 [8192, 4, 1024], P('ctx', ('dp', 'head')), may hold values from -3 to 3
- grad_out: bfloat16 [8192, 4, 1024], P('ctx', ('dp', 'head')), may hold values from -6 to 6
- doc_ids: int32 [8192], P('ctx'), may hold values from 0 to 3, never falling along the last dimension, each value on 1 to 4096 neighbouring positions
- owner: int32 [2048], P('ctx'), may hold values from 0 to 63, as said below
Outputs:
- grad_q_planned: bfloat16 [8192, 4, 1024], P('ctx', ('dp', 'head'))
- grad_k: bfloat16 [8192, 4, 128], P('ctx', ('dp', 'head'))
- grad_v: bfloat16 [8192, 4, 128], P('ctx', ('dp', 'head'))
The draws below stay inside these ranges and needn't reach their ends.
Inputs may be any that keep to these rules, and one draw needn't show every extreme that they name: `owner`: blocks b with the same b // 32 have different owners, and blocks with the same b % 32 have different owners, so every index of ctx owns exactly 32 blocks, one for each value of b % 32.
All inputs are finite; a program needn't handle non-finite values.
Results may differ from the reference program's by a relative error of at most 0.0047.
The reference program's roundings to bfloat16 on the way (of `probs_low`, `dscore` and `grad_q`) count: a program that leaves them out, or rounds other values in their place, can miss the bound.
Values may be sent and summed in bfloat16 or wider, within the bound.
No kernel may reach another device: no remote copies, remote signals or barrier semaphores. Data moves between devices by JAX's collectives and lax.ppermute only.
A program may use at most 64 MiB of HBM per device.

```python
import math
import jax
import jax.numpy as jnp
import numpy as np
from jax import lax

HD = 128
KVH = 4
GROUP = 8
TOK_DEV = 128
CPD = 32
L = 8192
BLK = 4
NBLK = 2048
DOCS = 4


def draw_keys(key, part):
    base = jax.random.normal(jax.random.fold_in(key, 31), (L, KVH, HD), jnp.float32)
    base = jnp.clip(base, -4.0, 4.0)
    return base.astype(jnp.bfloat16)


def draw_queries(key, part):
    base = jax.random.normal(jax.random.fold_in(key, 41), (L, KVH, GROUP * HD), jnp.float32)
    base = jnp.clip(base, -4.0, 4.0)
    return base.astype(jnp.bfloat16)


def draw_owner(key, part):
    peer_count = L // TOK_DEV
    per_device = TOK_DEV // BLK
    first = jax.random.permutation(jax.random.fold_in(key, 11), peer_count)
    second = jax.random.permutation(jax.random.fold_in(key, 12), peer_count)
    offsets = jax.random.permutation(jax.random.fold_in(key, 13), peer_count)[:per_device]
    block_ids = jnp.arange(NBLK, dtype=jnp.int32)
    anchor = block_ids // per_device
    local_slot = block_ids % per_device
    return first[(second[anchor] + offsets[local_slot]) % peer_count].astype(jnp.int32)


def shard_levels(stream_key, shape, cuts, low, high):
    level, own = 1.0, jax.random.fold_in(stream_key, 6)
    for axis_at, shards_of in cuts:
        heights = jnp.exp(jax.random.uniform(jax.random.fold_in(own, axis_at), (shards_of,), jnp.float32, low / len(cuts), high / len(cuts)))
        level = level * jnp.repeat(heights, shape[axis_at] // shards_of).reshape([-1 if axis == axis_at else 1 for axis in range(len(shape))])
    return level


def split_up(amount, total, reach, skew):
    loads = [(1 << 20) // math.isqrt(rank ** skew) + 1 for rank in range(2, amount + 1)]
    spare, counts = total - reach - (amount - 1), [1] * (amount - 1)
    while spare > 0:
        free = [i for i in range(amount - 1) if counts[i] < reach]
        mass, remaining = sum([loads[i] for i in free]), spare
        for i in free:
            addition = min(reach - counts[i], max(1, remaining * loads[i] // mass), spare)
            counts[i] = counts[i] + addition
            spare = spare - addition
    return np.array([reach] + counts)


def ragged_sizes(rng, number_of, total, reach, slope):
    if number_of == 2:
        one = jax.random.randint(rng, (), max(1, total - reach), min(reach, total - 1) + 1)
        return jnp.stack([one, total - one])
    sizes = jnp.asarray(split_up(number_of, total, reach, slope), jnp.int32)
    pairs = (number_of - 1) // 2
    donor, sink = sizes[1:1 + 2 * pairs:2], sizes[2:2 + 2 * pairs:2]
    margin = jnp.minimum(donor - 1, reach - sink)
    moved = jax.random.randint(jax.random.fold_in(rng, 1), (pairs,), 0, 1 << 20) % (margin + 1)
    sizes = sizes.at[1:1 + 2 * pairs:2].set(donor - moved).at[2:2 + 2 * pairs:2].set(sink + moved)
    return sizes[jax.random.permutation(jax.random.fold_in(rng, 2), number_of)]


def gaussian(stream_key, dims, spread, bound, split=(), kind=jnp.bfloat16):
    factor_of = shard_levels(stream_key, dims, split, -0.22, 0.18) if split else 1.0
    values = jax.random.normal(stream_key, dims, jnp.float32) * spread * factor_of
    return jnp.minimum(jnp.maximum(values, -bound), bound).astype(kind)


def setup_inputs(seed: int = 0) -> dict:
    key_list = jax.random.split(jax.random.key(seed), 8)
    queries = draw_queries(jax.random.fold_in(key_list[7], 71), 0)
    keys = draw_keys(jax.random.fold_in(key_list[7], 71), 0)
    values = gaussian(key_list[2], (L, KVH, HD), 1.0, 6.0, ((0, 256),))
    outputs = gaussian(key_list[3], (L, KVH, GROUP * HD), 0.5, 3.0, ((0, 64), (1, 4)))
    grad_out = gaussian(key_list[4], (L, KVH, GROUP * HD), 1.0, 6.0, ((0, 64), (1, 4)))
    doc_ids = jnp.searchsorted(jnp.cumsum(ragged_sizes(key_list[5], DOCS, L, L // 2, 0)), jnp.arange(L), side="right").astype(jnp.int32)
    owner = draw_owner(jax.random.fold_in(key_list[7], 71), 0)
    return {"queries": queries, "keys": keys, "values": values, "outputs": outputs, "grad_out": grad_out, "doc_ids": doc_ids, "owner": owner}


def reference(queries, keys, values, outputs, grad_out, doc_ids, owner):
    scale_val = HD ** -0.5
    q_block = min(256, L)
    block_total = L // q_block
    positions = jnp.arange(L, dtype=jnp.int32)
    high = lax.Precision.HIGHEST
    q_heads = jnp.transpose(queries, (1, 0, 2)).reshape(KVH, L, GROUP, HD)
    o_heads = jnp.transpose(outputs, (1, 0, 2)).reshape(KVH, L, GROUP, HD)
    do_heads = jnp.transpose(grad_out, (1, 0, 2)).reshape(KVH, L, GROUP, HD)
    k_heads = jnp.transpose(keys, (1, 0, 2))
    v_heads = jnp.transpose(values, (1, 0, 2))

    def per_group(members):
        q_grp, k_grp, v_grp, o_grp, do_grp = members
        k_full = k_grp.astype(jnp.float32)
        v_full = v_grp.astype(jnp.float32)

        def per_block(state, block_index):
            dk_sum, dv_sum = state
            row_start = block_index * q_block
            q_rows = lax.dynamic_slice_in_dim(q_grp, row_start, q_block, 0).astype(jnp.float32)
            do_rows = lax.dynamic_slice_in_dim(do_grp, row_start, q_block, 0).astype(jnp.float32)
            o_rows = lax.dynamic_slice_in_dim(o_grp, row_start, q_block, 0).astype(jnp.float32)
            row_pos = row_start + jnp.arange(q_block, dtype=jnp.int32)
            row_doc = lax.dynamic_slice_in_dim(doc_ids, row_start, q_block, 0)
            visible = ((doc_ids[None, :] == row_doc[:, None]) & (positions[None, :] <= row_pos[:, None]))[None]
            scores = jnp.einsum("rid,kd->irk", q_rows, k_full, precision=high) * scale_val
            peak = jnp.max(jnp.where(visible, scores, -jnp.inf), axis=-1, keepdims=True)
            total = jnp.sum(jnp.where(visible, jnp.exp(scores - peak), 0.0), axis=-1, keepdims=True)
            lse = peak + jnp.log(total)
            probs = jnp.where(visible, jnp.exp(scores - lse), 0.0)
            probs_low = probs.astype(jnp.bfloat16)
            dprob = jnp.einsum("rid,kd->irk", do_rows, v_full, precision=high)
            delta = jnp.transpose(jnp.sum(do_rows * o_rows, axis=-1), (1, 0))[..., None]
            dscore = (probs * (dprob - delta) * scale_val).astype(jnp.bfloat16)
            ds_wide = dscore.astype(jnp.float32)
            dq_rows = jnp.einsum("irk,kd->rid", ds_wide, k_full, precision=high)
            dk_sum = dk_sum + jnp.einsum("irk,rid->kd", ds_wide, q_rows, precision=high)
            dv_sum = dv_sum + jnp.einsum("irk,rid->kd", probs_low.astype(jnp.float32), do_rows, precision=high)
            return (dk_sum, dv_sum), dq_rows.astype(jnp.bfloat16)

        zeros_kd = jnp.zeros((L, HD), jnp.float32)
        (dk_grp, dv_grp), dq_blocks = lax.scan(per_block, (zeros_kd, zeros_kd), jnp.arange(block_total, dtype=jnp.int32))
        return dq_blocks.reshape(L, GROUP * HD), dk_grp, dv_grp

    dq_all, dk_all, dv_all = lax.map(per_group, (q_heads, k_heads, v_heads, o_heads, do_heads))
    grad_q = jnp.transpose(dq_all, (1, 0, 2))
    blocks = grad_q.reshape(NBLK, BLK, KVH, GROUP * HD)
    target = owner * CPD + jnp.arange(NBLK, dtype=jnp.int32) % CPD
    planned = jnp.zeros_like(blocks).at[target].set(blocks).reshape(L, KVH, GROUP * HD)
    grad_k = jnp.transpose(dk_all, (1, 0, 2)).astype(jnp.bfloat16)
    grad_v = jnp.transpose(dv_all, (1, 0, 2)).astype(jnp.bfloat16)
    return planned, grad_k, grad_v
```

```python
import functools

import jax
import jax.numpy as jnp
from jax import lax
from jax.experimental import pallas as pl
from jax.experimental.pallas import tpu as pltpu
from jax.sharding import Mesh, PartitionSpec as P

NEG_FILL = -1e30
BF = jnp.bfloat16
F32 = jnp.float32
EXTRA = 8


def nt(a, b):
    return lax.dot_general(a, b, (((1,), (1,)), ((), ())), preferred_element_type=F32)


def nn(a, b):
    return lax.dot_general(a, b, (((1,), (0,)), ((), ())), preferred_element_type=F32)


def tn(a, b):
    return lax.dot_general(a, b, (((0,), (0,)), ((), ())), preferred_element_type=F32)


def attention_kernel(
    place_ref,
    q_ref,
    do_ref,
    o_ref,
    doc_ref,
    own_ref,
    other_ref,
    dq_ref,
    own_grad_ref,
    other_grad_ref,
    q_all,
    do_all,
    p_all,
    peaks,
    state,
    dq_sum,
    *,
    zs,
    slots,
    scale,
    tile,
):
    rows, width = q_ref.shape
    hd = own_ref.shape[2] // 2
    heads = width // hd
    total = heads * rows
    chips = slots * zs
    x, z, core = place_ref[0], place_ref[1], place_ref[2]
    base = place_ref[3]
    exist = place_ref[4]
    here = (slots - 1) * zs + z

    def add_counts(j, tot):
        return (
            tot
            + own_ref[j, rows : rows + EXTRA, :].astype(F32)
            + other_ref[j, rows : rows + EXTRA, :].astype(F32)
        )

    counts = lax.fori_loop(0, chips, add_counts, jnp.zeros((EXTRA, 2 * hd), F32))
    doc = doc_ref[...]
    first_row = jnp.zeros((1, rows), F32)
    for d in range(1, EXTRA):
        first_row = jnp.where(doc == d, counts[d : d + 1, :rows], first_row)
    first_row = first_row.astype(jnp.int32) + exist
    lo_key = jnp.min(first_row)
    lo = jnp.maximum((lo_key - base) // (2 * rows), 0)
    q_pos = base + (here * 2 + core) * rows + lax.broadcasted_iota(jnp.int32, (1, rows), 1)
    firsts = jnp.concatenate([first_row] * (tile // rows), axis=1)
    lasts = jnp.concatenate([q_pos] * (tile // rows), axis=1)

    deltas = []
    for n in range(heads):
        cols = slice(n * hd, (n + 1) * hd)
        q_all[n * rows : (n + 1) * rows, :] = q_ref[:, cols]
        do_all[n * rows : (n + 1) * rows, :] = do_ref[:, cols]
        prod = do_ref[:, cols].astype(F32) * o_ref[:, cols].astype(F32)
        state[2:3, n * rows : (n + 1) * rows] = jnp.sum(prod.T, axis=0, keepdims=True)
    state[0:1, :] = jnp.full((1, total), NEG_FILL, F32)
    state[1:2, :] = jnp.zeros((1, total), F32)
    dq_sum[...] = jnp.zeros_like(dq_sum)

    key_iota = lax.broadcasted_iota(jnp.int32, (rows, tile), 0)

    def see(j, c, s):
        key_pos = key_iota + (base + (j * 2 + c) * rows)
        return jnp.where((key_pos >= firsts) & (key_pos <= lasts), s, NEG_FILL)

    def first_pass(j, carry):
        slot = j - lo
        k_own = own_ref[j, :rows, :hd]
        k_other = other_ref[j, :rows, :hd]
        for t in range(total // tile):
            cols = slice(t * tile, (t + 1) * tile)
            q_t = q_all[cols, :]
            s_own = see(j, core, nt(k_own, q_t))
            s_other = see(j, 1 - core, nt(k_other, q_t))
            old = state[0:1, cols]
            peak = jnp.maximum(
                old,
                jnp.maximum(
                    jnp.max(s_own, axis=0, keepdims=True), jnp.max(s_other, axis=0, keepdims=True)
                ),
            )
            p_own = jnp.exp((s_own - peak) * scale)
            p_other = jnp.exp((s_other - peak) * scale)
            p_all[slot, :rows, cols] = p_own
            p_all[slot, rows:, cols] = p_other
            state[1:2, cols] = (
                state[1:2, cols] * jnp.exp((old - peak) * scale)
                + jnp.sum(p_own, axis=0, keepdims=True)
                + jnp.sum(p_other, axis=0, keepdims=True)
            )
            state[0:1, cols] = peak
            peaks[slot, 0:1, cols] = peak
        return carry

    lax.fori_loop(lo, here + 1, first_pass, 0)
    state[1:2, :] = 1.0 / state[1:2, :]

    def second_pass(j, carry):
        slot = j - lo
        k_own = own_ref[j, :rows, :hd]
        k_other = other_ref[j, :rows, :hd]
        kk = jnp.concatenate([k_own, k_other], axis=0)
        vv = jnp.concatenate([own_ref[j, :rows, hd:], other_ref[j, :rows, hd:]], axis=0)
        dk = jnp.zeros((2 * rows, hd), F32)
        dv = jnp.zeros((2 * rows, hd), F32)
        for t in range(total // tile):
            cols = slice(t * tile, (t + 1) * tile)
            do_t = do_all[cols, :]
            factor = jnp.exp((peaks[slot, 0:1, cols] - state[0:1, cols]) * scale) * state[1:2, cols]
            probs = p_all[slot, :, cols] * factor
            dprob = nt(vv, do_t)
            dscore = (probs * (dprob - state[2:3, cols]) * scale).astype(BF)
            dv = dv + nn(probs.astype(BF), do_t)
            dk = dk + nn(dscore, q_all[cols, :])
            dq_sum[:, cols] += tn(kk, dscore)
        own_grad_ref[j, :, :hd] = dk[:rows]
        own_grad_ref[j, :, hd:] = dv[:rows]
        other_grad_ref[j, :, :hd] = dk[rows:]
        other_grad_ref[j, :, hd:] = dv[rows:]
        return carry

    lax.fori_loop(lo, here + 1, second_pass, 0)

    def clear(j, carry):
        own_grad_ref[j] = jnp.zeros((rows, 2 * hd), F32)
        other_grad_ref[j] = jnp.zeros((rows, 2 * hd), F32)
        return carry

    lax.fori_loop(0, lo, clear, 0)
    lax.fori_loop(here + 1, chips, clear, 0)
    for n in range(heads):
        dq_ref[:, n * hd : (n + 1) * hd] = dq_sum[:, n * rows : (n + 1) * rows].T.astype(BF)


def attention(place, q, do, o, doc, own, other, zs, slots, scale):
    rows, width = q.shape
    hd = own.shape[2] // 2
    total = rows * (width // hd)
    chips = slots * zs
    reach = (slots - 1) * zs + 1
    vmem = pl.BlockSpec(memory_space=pltpu.VMEM)
    return pl.pallas_call(
        functools.partial(
            attention_kernel, zs=zs, slots=slots, scale=scale, tile=min(256, total)
        ),
        in_specs=[pl.BlockSpec(memory_space=pltpu.SMEM)] + [vmem] * 6,
        out_specs=[vmem] * 3,
        out_shape=[
            jax.ShapeDtypeStruct((rows, width), BF),
            jax.ShapeDtypeStruct((chips, rows, 2 * hd), F32),
            jax.ShapeDtypeStruct((chips, rows, 2 * hd), F32),
        ],
        scratch_shapes=[
            pltpu.VMEM((total, hd), BF),
            pltpu.VMEM((total, hd), BF),
            pltpu.VMEM((reach, 2 * rows, total), F32),
            pltpu.VMEM((reach, 8, total), F32),
            pltpu.VMEM((8, total), F32),
            pltpu.VMEM((hd, total), F32),
        ],
        compiler_params=pltpu.CompilerParams(vmem_limit_bytes=56 * 1024 * 1024),
        name="attention_backward",
    )(place, q, do, o, doc, own, other)


def body(queries, keys, values, outputs, grad_out, doc_ids, owner):
    hd = keys.shape[2]
    scale = hd**-0.5
    rows, _, width = queries.shape
    xs, zs = lax.axis_size("x"), lax.axis_size("z")
    x, z, core = lax.axis_index("x"), lax.axis_index("z"), lax.axis_index("core")
    peers = xs * zs * 2
    slots = xs // 2 + 1
    per_device = owner.shape[0]
    block_len = rows // per_device

    near = lax.all_to_all(
        jnp.concatenate([keys, values], axis=-1), ("dp", "head"), split_axis=1, concat_axis=0, tiled=True
    )
    part = keys.shape[0]
    near = near.reshape(2, 2, part, 2 * hd).transpose(1, 0, 2, 3).reshape(rows, 2 * hd)
    earlier = jnp.sum(
        (doc_ids[None, :] < jnp.arange(EXTRA, dtype=jnp.int32)[:, None]).astype(F32), axis=1, keepdims=True
    )
    near = jnp.concatenate([near, jnp.broadcast_to(earlier, (EXTRA, 2 * hd)).astype(BF)], axis=0)

    line = lax.all_gather(near, "z", axis=0, tiled=False)
    shifted = [
        lax.ppermute(line, "x", [(i, i + s) for i in range(xs - s)]) for s in range(slots - 1, 0, -1)
    ]
    own = jnp.concatenate(shifted + [line], axis=0)
    other = lax.ppermute(own, "core", [(0, 1), (1, 0)])

    base = (x - (slots - 1)) * (zs * 2 * rows)
    place = jnp.stack([x, z, core, base, jnp.maximum(base, 0)]).astype(jnp.int32)
    dq, own_grad, other_grad = attention(
        place,
        queries.reshape(rows, width),
        grad_out.reshape(rows, width),
        outputs.reshape(rows, width),
        doc_ids.reshape(1, rows),
        own,
        other,
        zs,
        slots,
        scale,
    )

    swapped = lax.ppermute(other_grad, "core", [(0, 1), (1, 0)])
    summed = (own_grad + swapped).reshape(slots, zs, rows, 2 * hd)
    mine = summed[slots - 1]
    for s in range(1, slots):
        mine = mine + lax.ppermute(
            summed[slots - 1 - s].astype(BF), "x", [(i, i - s) for i in range(s, xs)]
        ).astype(F32)
    spread = lax.all_to_all(mine.astype(BF), "z", split_axis=0, concat_axis=0, tiled=True)
    grads = jnp.sum(spread.astype(F32), axis=0).astype(BF)
    grad_k = grads[:, None, :hd]
    grad_v = grads[:, None, hd:]

    slot_ids = jnp.arange(per_device, dtype=jnp.int32)
    send_mat = (owner[None, :] == jnp.arange(peers, dtype=jnp.int32)[:, None]).astype(BF)
    tags = jnp.broadcast_to((slot_ids + 1)[:, None, None], (per_device, block_len, 128)).astype(BF)
    blocks = jnp.concatenate([dq.reshape(per_device, block_len, width), tags], axis=-1)
    packed = jnp.einsum("pj,jbw->pbw", send_mat, blocks, preferred_element_type=F32).astype(BF)
    arrived = lax.all_to_all(packed, ("x", "z", "core"), split_axis=0, concat_axis=0, tiled=True)
    tag = arrived[:, 0, width].astype(jnp.int32)
    pick = (tag[None, :] == slot_ids[:, None] + 1).astype(BF)
    placed = jnp.einsum(
        "jp,pbw->jbw", pick, arrived[:, :, :width], preferred_element_type=F32
    ).astype(BF)
    return (placed.reshape(rows, 1, width), grad_k, grad_v)


def solution(mesh):
    sizes = mesh.shape
    dp, ctx, head = sizes["dp"], sizes["ctx"], sizes["head"]
    xs = 4
    fine = Mesh(
        mesh.devices.reshape(dp, xs, ctx // (2 * xs), 2, head), ("dp", "x", "z", "core", "head")
    )
    ctx_axes = ("x", "z", "core")
    heads = P(ctx_axes, ("dp", "head"), None)
    tokens = P(ctx_axes + ("head", "dp"), None, None)
    return jax.shard_map(
        body,
        mesh=fine,
        in_specs=(heads, tokens, tokens, heads, heads, P(ctx_axes), P(ctx_axes)),
        out_specs=(heads, heads, heads),
        check_vma=False,
    )
```

```python
import functools
import math

import jax
import jax.numpy as jnp
from jax import lax
from jax.experimental import pallas as pl
from jax.experimental.pallas import tpu as pltpu
from jax.sharding import Mesh, PartitionSpec as P


NEG_FILL = -1e30
BF = jnp.bfloat16
F32 = jnp.float32
EXTRA = 8


def nt(a, b):
    return lax.dot_general(a, b, (((1,), (1,)), ((), ())), preferred_element_type=F32)


def nn(a, b):
    return lax.dot_general(a, b, (((1,), (0,)), ((), ())), preferred_element_type=F32)


def stack_heads(dst, src):
    rows, width = src.shape
    hd = dst.shape[1]
    for n in range(width // hd):
        dst[n * rows : (n + 1) * rows, :] = src[:, n * hd : (n + 1) * hd]


def fill_window(win, own, other, far_own, far_other, z, zs):
    rows = win.shape[1] // 2
    for half, near, far in ((0, own, far_own), (1, other, far_other)):
        cut = pl.ds(half * rows, rows)
        for zz in range(zs):
            win[zs + zz, cut, :] = near[zz, 0, :rows, :]
            win[jnp.where(zz > z, zz, 2 * zs + zz), cut, :] = near[zz, 1, :rows, :]
        win[z, cut, :] = far


def out_index(j, z, zs):
    zz = lax.rem(j, zs)
    middle = (j >= zs) & (j < 2 * zs)
    return jnp.where(middle, 2 * zz, jnp.where(j == z, 2 * zs, 2 * zz + 1))


def softmax_kernel(
    place_ref,
    q_ref,
    do_ref,
    doc_ref,
    k_own,
    k_other,
    far_own,
    far_other,
    dv_own,
    dv_other,
    p_out,
    info_ref,
    q_all,
    do_all,
    k_win,
    p_all,
    peaks,
    state,
    sems,
    *,
    zs,
    scale,
    tile,
):
    rows, _ = q_ref.shape
    hd = q_all.shape[1]
    total = q_all.shape[0]
    x, z, core = place_ref[0], place_ref[1], place_ref[2]
    base, reach = place_ref[3], place_ref[4]
    here = 2 * zs + z
    unit = scale * math.log2(math.e)

    stack_heads(q_all, q_ref)
    stack_heads(do_all, do_ref)
    fill_window(k_win, k_own, k_other, far_own[:rows, :], far_other[:rows, :], z, zs)

    near_ok = (x >= 1).astype(F32)
    far_ok = (x >= 2).astype(F32)
    counts = (
        far_own[rows : rows + EXTRA, :].astype(F32) + far_other[rows : rows + EXTRA, :].astype(F32)
    ) * far_ok
    for zz in range(zs):
        both = k_own[zz, 0, rows : rows + EXTRA, :].astype(F32) + k_other[
            zz, 0, rows : rows + EXTRA, :
        ].astype(F32)
        counts = counts + both * near_ok
        both = k_own[zz, 1, rows : rows + EXTRA, :].astype(F32) + k_other[
            zz, 1, rows : rows + EXTRA, :
        ].astype(F32)
        counts = counts + both * jnp.where(zz > z, far_ok, 1.0)
    doc = doc_ref[...]
    first_row = jnp.zeros((1, rows), F32)
    for d in range(1, EXTRA):
        first_row = jnp.where(doc == d, counts[d : d + 1, :rows], first_row)
    first_row = first_row.astype(jnp.int32) + reach
    lo = (jnp.min(first_row) - base) // (2 * rows)
    edge = jnp.minimum((jnp.max(first_row) - base) // (2 * rows) + 1, here)
    info_ref[0] = lo
    q_pos = base + (here * 2 + core) * rows + lax.broadcasted_iota(jnp.int32, (1, rows), 1)
    firsts = jnp.concatenate([first_row] * (tile // rows), axis=1)
    lasts = jnp.concatenate([q_pos] * (tile // rows), axis=1)
    key_iota = lax.broadcasted_iota(jnp.int32, (rows, tile), 0)

    state[0:1, :] = jnp.full((1, total), NEG_FILL, F32)
    state[1:2, :] = jnp.zeros((1, total), F32)

    def visit(j, masked):
        slot = j - lo
        keys = k_win[j]
        for t in range(total // tile):
            cols = slice(t * tile, (t + 1) * tile)
            s = nt(keys, q_all[cols, :])
            if masked:
                pieces = []
                for half, c in ((0, core), (1, 1 - core)):
                    key_pos = key_iota + (base + (j * 2 + c) * rows)
                    pieces.append(
                        jnp.where(
                            (key_pos >= firsts) & (key_pos <= lasts),
                            s[half * rows : (half + 1) * rows],
                            NEG_FILL,
                        )
                    )
                s = jnp.concatenate(pieces, axis=0)
            old = state[0:1, cols]
            peak = jnp.maximum(old, jnp.max(s, axis=0, keepdims=True))
            p = jnp.exp2(s * unit - peak * unit)
            p_all[slot, :, cols] = p
            state[1:2, cols] = state[1:2, cols] * jnp.exp2((old - peak) * unit) + jnp.sum(
                p, axis=0, keepdims=True
            )
            state[0:1, cols] = peak
            peaks[slot, 0:1, cols] = peak

    def plain(j, carry):
        visit(j, False)
        return carry

    def edges(i, carry):
        visit(jnp.where(lo + i < edge, lo + i, here), True)
        return carry

    lax.fori_loop(0, edge - lo + 1, edges, 0)
    lax.fori_loop(edge, here, plain, 0)
    state[1:2, :] = 1.0 / state[1:2, :]

    def copy_out(slot):
        return pltpu.make_async_copy(p_all.at[slot], p_out.at[slot], sems.at[slot])

    def second(j, carry):
        slot = j - lo
        dv = jnp.zeros((2 * rows, hd), F32)
        for t in range(total // tile):
            cols = slice(t * tile, (t + 1) * tile)
            factor = jnp.exp2((peaks[slot, 0:1, cols] - state[0:1, cols]) * unit) * state[1:2, cols]
            probs = p_all[slot, :, cols] * factor
            p_all[slot, :, cols] = probs
            dv = dv + nn(probs.astype(BF), do_all[cols, :])
        copy_out(slot).start()
        at = out_index(j, z, zs)
        dv_own[at] = dv[:rows]
        dv_other[at] = dv[rows:]
        return carry

    lax.fori_loop(lo, here + 1, second, 0)

    def clear(j, carry):
        at = out_index(j, z, zs)
        dv_own[at] = jnp.zeros((rows, hd), F32)
        dv_other[at] = jnp.zeros((rows, hd), F32)
        return carry

    lax.fori_loop(z, lo, clear, 0)

    def finish(j, carry):
        copy_out(j - lo).wait()
        return carry

    lax.fori_loop(lo, here + 1, finish, 0)


def score_kernel(
    place_ref,
    info_ref,
    q_ref,
    do_ref,
    o_ref,
    k_own,
    k_other,
    far_own,
    far_other,
    v_own,
    v_other,
    far_v_own,
    far_v_other,
    p_in,
    dq_ref,
    dk_own,
    dk_other,
    q_all,
    do_all,
    k_win,
    v_win,
    p_all,
    delta,
    dq_sum,
    sems,
    *,
    zs,
    scale,
    tile,
):
    rows, width = q_ref.shape
    hd = q_all.shape[1]
    total = q_all.shape[0]
    z = place_ref[1]
    here = 2 * zs + z
    lo = info_ref[0]

    def copy_in(slot):
        return pltpu.make_async_copy(p_in.at[slot], p_all.at[slot], sems.at[slot])

    def begin(j, carry):
        copy_in(j - lo).start()
        return carry

    lax.fori_loop(lo, here + 1, begin, 0)
    stack_heads(q_all, q_ref)
    stack_heads(do_all, do_ref)
    fill_window(k_win, k_own, k_other, far_own[:rows, :], far_other[:rows, :], z, zs)
    fill_window(v_win, v_own, v_other, far_v_own[...], far_v_other[...], z, zs)
    for n in range(width // hd):
        cols = slice(n * hd, (n + 1) * hd)
        prod = do_ref[:, cols].astype(F32) * o_ref[:, cols].astype(F32)
        delta[0:1, n * rows : (n + 1) * rows] = jnp.sum(prod.T, axis=0, keepdims=True)
    dq_sum[...] = jnp.zeros_like(dq_sum)

    def clear(j, carry):
        at = out_index(j, z, zs)
        dk_own[at] = jnp.zeros((rows, hd), F32)
        dk_other[at] = jnp.zeros((rows, hd), F32)
        return carry

    lax.fori_loop(z, lo, clear, 0)

    def visit(j, carry):
        slot = j - lo
        copy_in(slot).wait()
        keys_t = k_win[j].T
        values = v_win[j]
        dk = jnp.zeros((2 * rows, hd), F32)
        for t in range(total // tile):
            cols = slice(t * tile, (t + 1) * tile)
            dprob = nt(values, do_all[cols, :])
            dscore = (p_all[slot, :, cols] * (dprob - delta[0:1, cols]) * scale).astype(BF)
            dk = dk + nn(dscore, q_all[cols, :])
            dq_sum[:, cols] += nn(keys_t, dscore)
        at = out_index(j, z, zs)
        dk_own[at] = dk[:rows]
        dk_other[at] = dk[rows:]
        return carry

    lax.fori_loop(lo, here + 1, visit, 0)
    for n in range(width // hd):
        dq_ref[:, n * hd : (n + 1) * hd] = dq_sum[:, n * rows : (n + 1) * rows].T.astype(BF)


def swap(value):
    return lax.ppermute(value, "core", [(0, 1), (1, 0)])


def reduce_blocks(own, other, zs, xs, z):
    rows, hd = own.shape[1:]
    both = own + swap(other)
    sent = both[: 2 * zs].astype(BF).reshape(zs, 2, rows, hd)
    came = lax.all_to_all(sent, "z", split_axis=0, concat_axis=0, tiled=True)
    came = came.astype(F32)
    later = (jnp.arange(zs) >= z)[:, None, None]
    mine = jnp.sum(jnp.where(later, came[:, 1], 0.0), axis=0)
    near = jnp.sum(came[:, 0], axis=0)
    far = jnp.sum(jnp.where(later, 0.0, came[:, 1]), axis=0) + both[2 * zs]
    from_next = lax.ppermute(near, "x", [(i, i - 1) for i in range(1, xs)])
    from_last = lax.ppermute(far, "x", [(i, i - 2) for i in range(2, xs)])
    return (mine + from_next + from_last).astype(BF)[:, None, :]


def program(queries, keys, values, outputs, grad_out, doc_ids, owner):
    hd = keys.shape[2]
    scale = hd**-0.5
    rows, _, width = queries.shape
    total = rows * (width // hd)
    tile = min(256, total)
    xs, zs = lax.axis_size("x"), lax.axis_size("z")
    x, z, core = lax.axis_index("x"), lax.axis_index("z"), lax.axis_index("core")
    peers = xs * zs * 2
    per_device = owner.shape[0]
    block_len = rows // per_device
    part = keys.shape[0]
    chips = 2 * zs + 1

    earlier = jnp.sum(
        (doc_ids[None, :] < jnp.arange(EXTRA, dtype=jnp.int32)[:, None]).astype(F32), axis=1, keepdims=True
    )
    earlier = jnp.broadcast_to(earlier[None], (4, EXTRA, 2 * hd)).astype(BF)
    mixed = jnp.transpose(jnp.concatenate([keys, values], axis=-1), (1, 0, 2))
    mixed = jnp.concatenate([mixed, earlier], axis=1)
    mixed = jnp.broadcast_to(mixed[:, None], (4, xs, part + EXTRA, 2 * hd))
    mixed = lax.all_to_all(
        mixed.reshape(4 * xs, part + EXTRA, 2 * hd),
        ("dp", "head", "x"),
        split_axis=0,
        concat_axis=0,
        tiled=True,
    ).reshape(2, 2, xs, part + EXTRA, 2 * hd)

    def piece(back):
        got = lax.dynamic_index_in_dim(mixed, lax.rem(x - back + xs, xs), 2, keepdims=False)
        tokens = jnp.transpose(got[:, :, :part], (1, 0, 2, 3)).reshape(rows, 2 * hd)
        return jnp.concatenate([tokens, got[0, 0, part:]], axis=0)

    last, near, far = piece(0), piece(1), piece(2)
    far_other = swap(far)

    def along_z(a, b, c):
        ahead = (jnp.arange(zs) >= z)[:, None, None]
        chosen = jnp.where(ahead, a[None], c[None])
        pair = jnp.stack([jnp.broadcast_to(b[None], chosen.shape), chosen], axis=1)
        return lax.all_to_all(pair, "z", split_axis=0, concat_axis=0, tiled=True)

    k_own = along_z(last[:, :hd], near[:, :hd], far[:, :hd])
    k_other = swap(k_own)
    v_own = along_z(last[:rows, hd:], near[:rows, hd:], far[:rows, hd:])

    base = (x - 2) * (zs * 2 * rows)
    place = jnp.stack([x, z, core, base, jnp.maximum(base + z * 2 * rows, 0)]).astype(jnp.int32)
    q = queries.reshape(rows, width)
    do = grad_out.reshape(rows, width)
    o = outputs.reshape(rows, width)
    vmem = pl.BlockSpec(memory_space=pltpu.VMEM)
    smem = pl.BlockSpec(memory_space=pltpu.SMEM)
    anywhere = pl.BlockSpec(memory_space=pl.ANY)
    grad_shape = jax.ShapeDtypeStruct((chips, rows, hd), F32)
    params = pltpu.CompilerParams(vmem_limit_bytes=48 * 1024 * 1024)
    dv_own, dv_other, probs, info = pl.pallas_call(
        functools.partial(softmax_kernel, zs=zs, scale=scale, tile=tile),
        in_specs=[smem] + [vmem] * 7,
        out_specs=[vmem, vmem, anywhere, smem],
        out_shape=[
            grad_shape,
            grad_shape,
            jax.ShapeDtypeStruct((chips, 2 * rows, total), F32),
            jax.ShapeDtypeStruct((1,), jnp.int32),
        ],
        scratch_shapes=[
            pltpu.VMEM((total, hd), BF),
            pltpu.VMEM((total, hd), BF),
            pltpu.VMEM((3 * zs, 2 * rows, hd), BF),
            pltpu.VMEM((chips, 2 * rows, total), F32),
            pltpu.VMEM((chips, 8, total), F32),
            pltpu.VMEM((8, total), F32),
            pltpu.SemaphoreType.DMA((chips,)),
        ],
        compiler_params=params,
        cost_estimate=pl.CostEstimate(
            flops=12_000_000_000, bytes_accessed=20_000_000, transcendentals=4_000_000
        ),
        name="softmax_and_value_gradient",
    )(
        place,
        q,
        do,
        doc_ids.reshape(1, rows),
        k_own,
        k_other,
        far[:, :hd],
        far_other[:, :hd],
    )
    v_other = swap(v_own)
    grad_v = reduce_blocks(dv_own, dv_other, zs, xs, z)
    dq, dk_own, dk_other = pl.pallas_call(
        functools.partial(score_kernel, zs=zs, scale=scale, tile=tile),
        in_specs=[smem, smem] + [vmem] * 11 + [anywhere],
        out_specs=[vmem] * 3,
        out_shape=[jax.ShapeDtypeStruct((rows, width), BF), grad_shape, grad_shape],
        scratch_shapes=[
            pltpu.VMEM((total, hd), BF),
            pltpu.VMEM((total, hd), BF),
            pltpu.VMEM((3 * zs, 2 * rows, hd), BF),
            pltpu.VMEM((3 * zs, 2 * rows, hd), BF),
            pltpu.VMEM((chips, 2 * rows, total), F32),
            pltpu.VMEM((8, total), F32),
            pltpu.VMEM((hd, total), F32),
            pltpu.SemaphoreType.DMA((chips,)),
        ],
        compiler_params=params,
        cost_estimate=pl.CostEstimate(
            flops=12_000_000_000, bytes_accessed=20_000_000, transcendentals=0
        ),
        name="score_gradient",
    )(
        place,
        info,
        q,
        do,
        o,
        k_own,
        k_other,
        far[:, :hd],
        far_other[:, :hd],
        v_own,
        v_other,
        far[:rows, hd:],
        far_other[:rows, hd:],
        probs,
    )
    grad_k = reduce_blocks(dk_own, dk_other, zs, xs, z)

    slot_ids = jnp.arange(per_device, dtype=jnp.int32)
    send_mat = (owner[None, :] == jnp.arange(peers, dtype=jnp.int32)[:, None]).astype(BF)
    tags = jnp.broadcast_to((slot_ids + 1)[:, None, None], (per_device, block_len, 128)).astype(BF)
    blocks = jnp.concatenate([dq.reshape(per_device, block_len, width), tags], axis=-1)
    packed = jnp.einsum("pj,jbw->pbw", send_mat, blocks, preferred_element_type=F32).astype(BF)
    arrived = lax.all_to_all(packed, ("x", "z", "core"), split_axis=0, concat_axis=0, tiled=True)
    tag = arrived[:, 0, width].astype(jnp.int32)
    pick = (tag[None, :] == slot_ids[:, None] + 1).astype(BF)
    placed = jnp.einsum(
        "jp,pbw->jbw", pick, arrived[:, :, :width], preferred_element_type=F32
    ).astype(BF)
    return (placed.reshape(rows, 1, width), grad_k, grad_v)


def solution(mesh):
    sizes = mesh.shape
    dp, ctx, head = sizes["dp"], sizes["ctx"], sizes["head"]
    xs = 4
    fine = Mesh(
        mesh.devices.reshape(dp, xs, ctx // (2 * xs), 2, head), ("dp", "x", "z", "core", "head")
    )
    ctx_axes = ("x", "z", "core")
    heads = P(ctx_axes, ("dp", "head"), None)
    tokens = P(ctx_axes + ("head", "dp"), None, None)
    return jax.shard_map(
        program,
        mesh=fine,
        in_specs=(heads, tokens, tokens, heads, heads, P(ctx_axes), P(ctx_axes)),
        out_specs=(heads, heads, heads),
        check_vma=False,
    )
```

```python
import functools
import math

import jax
import jax.numpy as jnp
from jax import lax
from jax.experimental import pallas as pl
from jax.experimental.pallas import tpu as pltpu
from jax.sharding import Mesh, PartitionSpec as P


NEG_FILL = -1e30
BF = jnp.bfloat16
F32 = jnp.float32
COUNTS = 4


def nt(a, b):
    return lax.dot_general(a, b, (((1,), (1,)), ((), ())), preferred_element_type=F32)


def nn(a, b):
    return lax.dot_general(a, b, (((1,), (0,)), ((), ())), preferred_element_type=F32)


def stack_heads(dst, src):
    rows, width = src.shape
    hd = dst.shape[1]
    for n in range(width // hd):
        dst[n * rows : (n + 1) * rows, :] = src[:, n * hd : (n + 1) * hd]


def fill_window(win, own, other, far_own, far_other, z, zs):
    rows = win.shape[1] // 2
    for half, near, far in ((0, own, far_own), (1, other, far_other)):
        cut = pl.ds(half * rows, rows)
        for zz in range(zs):
            win[zs + zz, cut, :] = near[zz, 0, :rows, :]
            win[jnp.where(zz > z, zz, 2 * zs + zz), cut, :] = near[zz, 1, :rows, :]
        win[z, cut, :] = far


def out_index(j, z, zs):
    zz = lax.rem(j, zs)
    middle = (j >= zs) & (j < 2 * zs)
    return jnp.where(middle, 2 * zz, jnp.where(j == z, 2 * zs, 2 * zz + 1))


def relative_index(j, z, zs):
    zz = lax.rem(lax.rem(j, zs) + zs - z, zs)
    middle = (j >= zs) & (j < 2 * zs)
    return jnp.where(middle, 2 * zz, jnp.where(j == z, 2 * zs, 2 * zz + 1))


def softmax_kernel(
    place_ref,
    q_ref,
    do_ref,
    doc_ref,
    k_own,
    k_other,
    far_own,
    far_other,
    dv_own,
    dv_other,
    p_out,
    info_ref,
    factors,
    q_all,
    do_all,
    k_win,
    p_all,
    raw,
    low,
    state,
    sems,
    *,
    zs,
    scale,
    tile,
    group,
):
    rows, _ = q_ref.shape
    hd = q_all.shape[1]
    total = q_all.shape[0]
    x, z, core = place_ref[0], place_ref[1], place_ref[2]
    base, reach = place_ref[3], place_ref[4]
    here = 2 * zs + z
    unit = scale * math.log2(math.e)

    stack_heads(q_all, q_ref)
    stack_heads(do_all, do_ref)
    fill_window(k_win, k_own, k_other, far_own[:rows, :], far_other[:rows, :], z, zs)

    near_ok = (x >= 1).astype(F32)
    far_ok = (x >= 2).astype(F32)
    counts = (
        far_own[rows : rows + COUNTS, :].astype(F32) + far_other[rows : rows + COUNTS, :].astype(F32)
    ) * far_ok
    for zz in range(zs):
        both = k_own[zz, 0, rows : rows + COUNTS, :].astype(F32) + k_other[
            zz, 0, rows : rows + COUNTS, :
        ].astype(F32)
        counts = counts + both * near_ok
        both = k_own[zz, 1, rows : rows + COUNTS, :].astype(F32) + k_other[
            zz, 1, rows : rows + COUNTS, :
        ].astype(F32)
        counts = counts + both * jnp.where(zz > z, far_ok, 1.0)
    doc = doc_ref[...]
    first_row = jnp.zeros((1, rows), F32)
    for d in range(1, COUNTS):
        first_row = jnp.where(doc == d, counts[d : d + 1, :rows], first_row)
    first_row = first_row.astype(jnp.int32) + reach
    lo = (jnp.min(first_row) - base) // (2 * rows)
    edge = jnp.minimum((jnp.max(first_row) - base) // (2 * rows) + 1, here)
    info_ref[0] = lo
    q_pos = base + (here * 2 + core) * rows + lax.broadcasted_iota(jnp.int32, (1, rows), 1)
    firsts = jnp.concatenate([first_row] * (tile // rows), axis=1)
    lasts = jnp.concatenate([q_pos] * (tile // rows), axis=1)
    key_iota = lax.broadcasted_iota(jnp.int32, (rows, tile), 0)

    state[0:1, :] = jnp.full((1, total), NEG_FILL, F32)
    state[1:2, :] = jnp.zeros((1, total), F32)

    def visit(j, masked):
        slot = j - lo
        for t in range(total // tile):
            cols = slice(t * tile, (t + 1) * tile)
            q_t = q_all[cols, :]
            peak = state[0:1, cols]
            for half in range(2):
                cut = slice(half * rows, (half + 1) * rows)
                s = nt(k_win[j, cut, :], q_t) * unit
                if masked:
                    key_pos = key_iota + (base + (j * 2 + (core if half == 0 else 1 - core)) * rows)
                    s = jnp.where((key_pos >= firsts) & (key_pos <= lasts), s, NEG_FILL)
                peak = jnp.maximum(peak, jnp.max(s, axis=0, keepdims=True))
                raw[cut, cols] = s
            factors[slot, 0:1, cols] = peak
        for t in range(total // tile):
            cols = slice(t * tile, (t + 1) * tile)
            old, peak = state[0:1, cols], factors[slot, 0:1, cols]
            seen = state[1:2, cols] * jnp.exp2(old - peak)
            for half in range(2):
                cut = slice(half * rows, (half + 1) * rows)
                p = jnp.exp2(raw[cut, cols] - peak)
                p_all[slot, cut, cols] = p
                seen = seen + jnp.sum(p, axis=0, keepdims=True)
            state[0:1, cols] = peak
            state[1:2, cols] = seen
        pltpu.make_async_copy(p_all.at[slot], p_out.at[slot], sems.at[slot]).start()

    def plain(j, carry):
        visit(j, False)
        return carry

    def edges(i, carry):
        visit(jnp.where(lo + i < edge, lo + i, here), True)
        return carry

    lax.fori_loop(0, edge - lo + 1, edges, 0)
    lax.fori_loop(edge, here, plain, 0)
    state[1:2, :] = 1.0 / state[1:2, :]

    def second(j, carry):
        slot = j - lo
        dv = jnp.zeros((2 * rows, hd), F32)
        for g in range(total // group):
            for t in range(g * group // tile, (g + 1) * group // tile):
                cols = slice(t * tile, (t + 1) * tile)
                factor = jnp.exp2(factors[slot, 0:1, cols] - state[0:1, cols]) * state[1:2, cols]
                factors[slot, 0:1, cols] = factor
                for half in range(2):
                    cut = slice(half * rows, (half + 1) * rows)
                    low[cut, cols] = (p_all[slot, cut, cols] * factor).astype(BF)
            span = slice(g * group, (g + 1) * group)
            dv = dv + nn(low[:, span], do_all[span, :])
        at = out_index(j, z, zs)
        dv_own[at] = dv[:rows]
        dv_other[at] = dv[rows:]
        return carry

    lax.fori_loop(lo, here + 1, second, 0)

    def clear(j, carry):
        at = out_index(j, z, zs)
        dv_own[at] = jnp.zeros((rows, hd), F32)
        dv_other[at] = jnp.zeros((rows, hd), F32)
        return carry

    lax.fori_loop(z, lo, clear, 0)

    def finish(j, carry):
        slot = j - lo
        pltpu.make_async_copy(p_all.at[slot], p_out.at[slot], sems.at[slot]).wait()
        return carry

    lax.fori_loop(lo, here + 1, finish, 0)


def score_kernel(
    place_ref,
    info_ref,
    q_ref,
    do_ref,
    o_ref,
    k_own,
    k_other,
    far_own,
    far_other,
    v_own,
    v_other,
    far_v_own,
    far_v_other,
    factors,
    owner_ref,
    p_in,
    packed_ref,
    dk_own,
    dk_other,
    q_all,
    do_all,
    k_win,
    v_win,
    p_all,
    low,
    delta,
    dq_sum,
    sems,
    *,
    zs,
    scale,
    tile,
    group,
    block,
):
    rows, width = q_ref.shape
    hd = q_all.shape[1]
    total = q_all.shape[0]
    z = place_ref[1]
    here = 2 * zs + z
    lo = info_ref[0]

    def copy_in(slot):
        return pltpu.make_async_copy(p_in.at[slot], p_all.at[slot], sems.at[slot])

    def begin(j, carry):
        copy_in(j - lo).start()
        return carry

    lax.fori_loop(lo, here + 1, begin, 0)
    stack_heads(q_all, q_ref)
    stack_heads(do_all, do_ref)
    fill_window(k_win, k_own, k_other, far_own[:rows, :], far_other[:rows, :], z, zs)
    fill_window(v_win, v_own, v_other, far_v_own[...], far_v_other[...], z, zs)
    for n in range(width // hd):
        cols = slice(n * hd, (n + 1) * hd)
        prod = do_ref[:, cols].astype(F32) * o_ref[:, cols].astype(F32)
        delta[0:1, n * rows : (n + 1) * rows] = jnp.sum(prod.T, axis=0, keepdims=True)
    dq_sum[...] = jnp.zeros_like(dq_sum)

    def clear(j, carry):
        at = relative_index(j, z, zs)
        dk_own[at] = jnp.zeros((rows, hd), F32)
        dk_other[at] = jnp.zeros((rows, hd), F32)
        return carry

    lax.fori_loop(z, lo, clear, 0)

    def visit(j, carry):
        slot = j - lo
        copy_in(slot).wait()
        keys_t = k_win[j].T
        dk = jnp.zeros((2 * rows, hd), F32)
        for g in range(total // group):
            for t in range(g * group // tile, (g + 1) * group // tile):
                cols = slice(t * tile, (t + 1) * tile)
                do_t = do_all[cols, :]
                for half in range(2):
                    cut = slice(half * rows, (half + 1) * rows)
                    dprob = nt(v_win[j, cut, :], do_t)
                    probs = p_all[slot, cut, cols] * factors[slot, 0:1, cols]
                    low[cut, cols] = (probs * (dprob - delta[0:1, cols]) * scale).astype(BF)
            span = slice(g * group, (g + 1) * group)
            dk = dk + nn(low[:, span], q_all[span, :])
            dq_sum[:, span] += nn(keys_t, low[:, span])
        at = relative_index(j, z, zs)
        dk_own[at] = dk[:rows]
        dk_other[at] = dk[rows:]
        return carry

    lax.fori_loop(lo, here + 1, visit, 0)
    half_width = width // 2
    half_heads = half_width // hd
    spots = packed_ref.shape[0]
    row = lax.broadcasted_iota(jnp.int32, (spots, rows), 0)
    token = lax.broadcasted_iota(jnp.int32, (spots, rows), 1)
    goes = (row // (2 * block) == owner_ref[...]) & (row % block == token % block)
    packed = jnp.zeros((spots, half_width), F32)
    for h in range(2):
        here_half = goes & (row // block % 2 == h)
        turned = [
            dq_sum[:, n * rows : (n + 1) * rows].T.astype(BF)
            for n in range(h * half_heads, (h + 1) * half_heads)
        ]
        packed = packed + nn(here_half.astype(F32).astype(BF), jnp.concatenate(turned, axis=1))
    packed_ref[...] = packed.astype(BF)


def swap(value):
    return lax.ppermute(value, "core", [(0, 1), (1, 0)])


def placement_kernel(place_ref, owners_ref, arrived_ref, out_ref, *, block):
    peers, per_device = owners_ref.shape
    rows, spots = out_ref.shape[0], arrived_ref.shape[0]
    half_width = arrived_ref.shape[1]
    hit = (owners_ref[...].astype(F32) == place_ref[5].astype(F32)).astype(F32).astype(BF)
    slot = lax.broadcasted_iota(jnp.int32, (rows, per_device), 0) // block
    to_rows = (slot == lax.broadcasted_iota(jnp.int32, (rows, per_device), 1)).astype(F32).astype(BF)
    peer = lax.broadcasted_iota(jnp.int32, (peers, spots), 1) // (2 * block)
    to_spots = (peer == lax.broadcasted_iota(jnp.int32, (peers, spots), 0)).astype(F32).astype(BF)
    pick = nn(nt(to_rows, hit).astype(BF), to_spots)
    row = lax.broadcasted_iota(jnp.int32, (rows, spots), 0)
    spot = lax.broadcasted_iota(jnp.int32, (rows, spots), 1)
    same = spot % block == row % block
    for h in range(2):
        chosen = jnp.where(same & (spot // block % 2 == h), pick, 0.0).astype(BF)
        out_ref[:, h * half_width : (h + 1) * half_width] = nn(chosen, arrived_ref[...]).astype(BF)


def along_x(mine, near, far, xs):
    from_next = lax.ppermute(near, "x", [(i, i - 1) for i in range(1, xs)])
    from_last = lax.ppermute(far, "x", [(i, i - 2) for i in range(2, xs)])
    return (mine + from_next + from_last).astype(BF)[:, None, :]


def reduce_at_once(own, other, zs, xs, z):
    rows, hd = own.shape[1:]
    swapped = swap(other)
    sent = (own[: 2 * zs] + swapped[: 2 * zs]).astype(BF).reshape(zs, 2, rows, hd)
    came = lax.all_to_all(sent, "z", split_axis=0, concat_axis=0, tiled=True)
    came = came.astype(F32)
    later = (jnp.arange(zs) >= z)[:, None, None]
    mine = jnp.sum(jnp.where(later, came[:, 1], 0.0), axis=0)
    near = jnp.sum(came[:, 0], axis=0)
    far = jnp.sum(jnp.where(later, 0.0, came[:, 1]), axis=0) + own[2 * zs] + swapped[2 * zs]
    return along_x(mine, near, far, xs)


def reduce_by_shifts(own, other, zs, xs, z):
    swapped = swap(other)
    came = []
    for k in range(1, zs):
        sent = (own[2 * k : 2 * k + 2] + swapped[2 * k : 2 * k + 2]).astype(BF)
        came.append(lax.ppermute(sent, "z", [(i, (i + k) % zs) for i in range(zs)]))
    mine = own[1] + swapped[1]
    near = own[0] + swapped[0]
    far = own[2 * zs] + swapped[2 * zs]
    for k, got in enumerate(came, 1):
        near = near + got[0].astype(F32)
        mine = mine + jnp.where(z < k, got[1].astype(F32), 0.0)
        far = far + jnp.where(z < k, 0.0, got[1].astype(F32))
    return along_x(mine, near, far, xs)


def program(queries, keys, values, outputs, grad_out, doc_ids, owner):
    hd = keys.shape[2]
    scale = hd**-0.5
    rows, _, width = queries.shape
    total = rows * (width // hd)
    tile = min(256, total)
    group = min(512, total)
    xs, zs = lax.axis_size("x"), lax.axis_size("z")
    x, z, core = lax.axis_index("x"), lax.axis_index("z"), lax.axis_index("core")
    peers = xs * zs * 2
    per_device = owner.shape[0]
    block_len = rows // per_device
    part = keys.shape[0]
    chips = 2 * zs + 1

    extra = COUNTS + xs
    earlier = jnp.sum(
        (doc_ids[None, :] < jnp.arange(COUNTS, dtype=jnp.int32)[:, None]).astype(F32), axis=1, keepdims=True
    )
    notes = jnp.concatenate(
        [
            jnp.broadcast_to(earlier, (COUNTS, 2 * hd)),
            jnp.broadcast_to(jnp.pad(owner.astype(F32), (0, 2 * hd - per_device)), (xs, 2 * hd)),
        ],
        axis=0,
    ).astype(BF)
    mixed = jnp.transpose(jnp.concatenate([keys, values], axis=-1), (1, 0, 2))
    mixed = jnp.concatenate([mixed, jnp.broadcast_to(notes[None], (4, extra, 2 * hd))], axis=1)
    mixed = jnp.broadcast_to(mixed[:, None], (4, xs, part + extra, 2 * hd))
    mixed = lax.all_to_all(
        mixed.reshape(4 * xs, part + extra, 2 * hd),
        ("dp", "head", "x"),
        split_axis=0,
        concat_axis=0,
        tiled=True,
    ).reshape(2, 2, xs, part + extra, 2 * hd)

    def piece(back):
        got = lax.dynamic_index_in_dim(mixed, lax.rem(x - back + xs, xs), 2, keepdims=False)
        tokens = jnp.transpose(got[:, :, :part], (1, 0, 2, 3)).reshape(rows, 2 * hd)
        return jnp.concatenate([tokens, got[0, 0, part:]], axis=0)

    last, near, far = piece(0), piece(1), piece(2)
    far_other = swap(far)

    def along_z(a, b, c):
        ahead = (jnp.arange(zs) >= z)[:, None, None]
        chosen = jnp.where(ahead, a[None], c[None])
        pair = jnp.stack([jnp.broadcast_to(b[None], chosen.shape), chosen], axis=1)
        return lax.all_to_all(pair, "z", split_axis=0, concat_axis=0, tiled=True)

    held = mixed[0, 0, :, part + COUNTS, :hd]
    near_keys = jnp.concatenate([near[: rows + COUNTS, :hd], held], axis=0)
    k_own = along_z(last[:, :hd], near_keys, far[:, :hd])
    k_other = swap(k_own)
    v_own = along_z(last[:rows, hd:], near[:rows, hd:], far[:rows, hd:])

    base = (x - 2) * (zs * 2 * rows)
    me = (x * zs + z) * 2 + core
    place = jnp.stack([x, z, core, base, jnp.maximum(base + z * 2 * rows, 0), me]).astype(jnp.int32)
    q = queries.reshape(rows, width)
    do = grad_out.reshape(rows, width)
    o = outputs.reshape(rows, width)
    vmem = pl.BlockSpec(memory_space=pltpu.VMEM)
    smem = pl.BlockSpec(memory_space=pltpu.SMEM)
    anywhere = pl.BlockSpec(memory_space=pl.ANY)
    grad_shape = jax.ShapeDtypeStruct((chips, rows, hd), F32)
    params = pltpu.CompilerParams(vmem_limit_bytes=48 * 1024 * 1024)
    dv_own, dv_other, probs, info, factors = pl.pallas_call(
        functools.partial(softmax_kernel, zs=zs, scale=scale, tile=tile, group=group),
        in_specs=[smem] + [vmem] * 7,
        out_specs=[vmem, vmem, anywhere, smem, vmem],
        out_shape=[
            grad_shape,
            grad_shape,
            jax.ShapeDtypeStruct((chips, 2 * rows, total), F32),
            jax.ShapeDtypeStruct((1,), jnp.int32),
            jax.ShapeDtypeStruct((chips, 8, total), F32),
        ],
        scratch_shapes=[
            pltpu.VMEM((total, hd), BF),
            pltpu.VMEM((total, hd), BF),
            pltpu.VMEM((3 * zs, 2 * rows, hd), BF),
            pltpu.VMEM((chips, 2 * rows, total), F32),
            pltpu.VMEM((2 * rows, total), F32),
            pltpu.VMEM((2 * rows, total), BF),
            pltpu.VMEM((8, total), F32),
            pltpu.SemaphoreType.DMA((chips,)),
        ],
        compiler_params=params,
        cost_estimate=pl.CostEstimate(
            flops=12_000_000_000, bytes_accessed=20_000_000, transcendentals=4_000_000
        ),
        name="softmax_and_value_gradient",
    )(
        place,
        q,
        do,
        doc_ids.reshape(1, rows),
        k_own,
        k_other,
        far[:, :hd],
        far_other[:, :hd],
    )
    v_other = swap(v_own)
    grad_v = reduce_at_once(dv_own, dv_other, zs, xs, z)
    packed, dk_own, dk_other = pl.pallas_call(
        functools.partial(
            score_kernel, zs=zs, scale=scale, tile=tile, group=group, block=block_len
        ),
        in_specs=[smem, smem] + [vmem] * 13 + [anywhere],
        out_specs=[vmem] * 3,
        out_shape=[
            jax.ShapeDtypeStruct((peers * 2 * block_len, width // 2), BF),
            grad_shape,
            grad_shape,
        ],
        scratch_shapes=[
            pltpu.VMEM((total, hd), BF),
            pltpu.VMEM((total, hd), BF),
            pltpu.VMEM((3 * zs, 2 * rows, hd), BF),
            pltpu.VMEM((3 * zs, 2 * rows, hd), BF),
            pltpu.VMEM((chips, 2 * rows, total), F32),
            pltpu.VMEM((2 * rows, total), BF),
            pltpu.VMEM((8, total), F32),
            pltpu.VMEM((hd, total), F32),
            pltpu.SemaphoreType.DMA((chips,)),
        ],
        compiler_params=params,
        cost_estimate=pl.CostEstimate(
            flops=12_000_000_000, bytes_accessed=20_000_000, transcendentals=0
        ),
        name="score_gradient",
    )(
        place,
        info,
        q,
        do,
        o,
        k_own,
        k_other,
        far[:, :hd],
        far_other[:, :hd],
        v_own,
        v_other,
        far[:rows, hd:],
        far_other[:rows, hd:],
        factors,
        jnp.repeat(owner, block_len)[None],
        probs,
    )
    grad_k = reduce_by_shifts(dk_own, dk_other, zs, xs, z)

    seen = [k[:, 0, rows + COUNTS :, :per_device] for k in (k_own, k_other)]
    even = jnp.where(core == 0, seen[0], seen[1])
    odd = jnp.where(core == 0, seen[1], seen[0])
    owners = jnp.transpose(jnp.stack([even, odd], axis=2), (1, 0, 2, 3)).reshape(peers, per_device)
    arrived = lax.all_to_all(
        packed.reshape(peers, 2 * block_len, width // 2),
        ("x", "z", "core"),
        split_axis=0,
        concat_axis=0,
        tiled=True,
    )
    placed = pl.pallas_call(
        functools.partial(placement_kernel, block=block_len),
        in_specs=[smem, vmem, vmem],
        out_specs=vmem,
        out_shape=jax.ShapeDtypeStruct((rows, width), BF),
        name="query_gradient_placement",
    )(place, owners, arrived.reshape(packed.shape))
    return (placed.reshape(rows, 1, width), grad_k, grad_v)


def solution(mesh):
    sizes = mesh.shape
    dp, ctx, head = sizes["dp"], sizes["ctx"], sizes["head"]
    xs = 4
    fine = Mesh(
        mesh.devices.reshape(dp, xs, ctx // (2 * xs), 2, head), ("dp", "x", "z", "core", "head")
    )
    ctx_axes = ("x", "z", "core")
    heads = P(ctx_axes, ("dp", "head"), None)
    tokens = P(ctx_axes + ("head", "dp"), None, None)
    return jax.shard_map(
        program,
        mesh=fine,
        in_specs=(heads, tokens, tokens, heads, heads, P(ctx_axes), P(ctx_axes)),
        out_specs=(heads, heads, heads),
        check_vma=False,
    )
```

```python
import functools
import math

import jax
import jax.numpy as jnp
from jax import lax
from jax.experimental import pallas as pl
from jax.experimental.pallas import tpu as pltpu
from jax.sharding import Mesh, PartitionSpec as P


NEG_FILL = -1e30
VMEM_BYTES = 60 * 1024 * 1024
BF = jnp.bfloat16
F32 = jnp.float32
COUNTS = 4


def nt(a, b):
    return lax.dot_general(a, b, (((1,), (1,)), ((), ())), preferred_element_type=F32)


def nn(a, b):
    return lax.dot_general(a, b, (((1,), (0,)), ((), ())), preferred_element_type=F32)


def stack_heads(dst, src):
    rows, width = src.shape
    hd = dst.shape[1]
    for n in range(width // hd):
        dst[n * rows : (n + 1) * rows, :] = src[:, n * hd : (n + 1) * hd]


def fill_window(win, own, other, far_own, far_other, z, zs):
    rows = win.shape[1] // 2
    for half, near, far in ((0, own, far_own), (1, other, far_other)):
        cut = pl.ds(half * rows, rows)
        for zz in range(zs):
            win[zs + zz, cut, :] = near[zz, 0, :rows, :]
            win[jnp.where(zz > z, zz, 2 * zs + zz), cut, :] = near[zz, 1, :rows, :]
        win[z, cut, :] = far


def out_index(j, z, zs):
    zz = lax.rem(j, zs)
    middle = (j >= zs) & (j < 2 * zs)
    return jnp.where(middle, 2 * zz, jnp.where(j == z, 2 * zs, 2 * zz + 1))


def relative_index(j, z, zs):
    zz = lax.rem(lax.rem(j, zs) + zs - z, zs)
    middle = (j >= zs) & (j < 2 * zs)
    return jnp.where(middle, 2 * zz, jnp.where(j == z, 2 * zs, 2 * zz + 1))


def softmax_kernel(
    place_ref,
    q_ref,
    do_ref,
    doc_ref,
    k_own,
    k_other,
    far_own,
    far_other,
    dv_own,
    dv_other,
    p_out,
    info_ref,
    factors,
    q_all,
    do_all,
    k_win,
    p_all,
    raw,
    low,
    state,
    sems,
    *,
    zs,
    scale,
    tile,
    group,
):
    rows, _ = q_ref.shape
    hd = q_all.shape[1]
    total = q_all.shape[0]
    x, z, core = place_ref[0], place_ref[1], place_ref[2]
    base, reach = place_ref[3], place_ref[4]
    here = 2 * zs + z
    unit = scale * math.log2(math.e)

    stack_heads(q_all, q_ref)
    stack_heads(do_all, do_ref)
    fill_window(k_win, k_own, k_other, far_own[:rows, :], far_other[:rows, :], z, zs)

    near_ok = (x >= 1).astype(F32)
    far_ok = (x >= 2).astype(F32)
    counts = (
        far_own[rows : rows + COUNTS, :].astype(F32) + far_other[rows : rows + COUNTS, :].astype(F32)
    ) * far_ok
    for zz in range(zs):
        both = k_own[zz, 0, rows : rows + COUNTS, :].astype(F32) + k_other[
            zz, 0, rows : rows + COUNTS, :
        ].astype(F32)
        counts = counts + both * near_ok
        both = k_own[zz, 1, rows : rows + COUNTS, :].astype(F32) + k_other[
            zz, 1, rows : rows + COUNTS, :
        ].astype(F32)
        counts = counts + both * jnp.where(zz > z, far_ok, 1.0)
    doc = doc_ref[...]
    first_row = jnp.zeros((1, rows), F32)
    for d in range(1, COUNTS):
        first_row = jnp.where(doc == d, counts[d : d + 1, :rows], first_row)
    first_row = first_row.astype(jnp.int32) + reach
    lo = (jnp.min(first_row) - base) // (2 * rows)
    edge = jnp.minimum((jnp.max(first_row) - base) // (2 * rows) + 1, here)
    info_ref[0] = lo
    q_pos = base + (here * 2 + core) * rows + lax.broadcasted_iota(jnp.int32, (1, rows), 1)
    firsts = jnp.concatenate([first_row] * (tile // rows), axis=1)
    lasts = jnp.concatenate([q_pos] * (tile // rows), axis=1)
    key_iota = lax.broadcasted_iota(jnp.int32, (rows, tile), 0)

    state[0:1, :] = jnp.full((1, total), NEG_FILL, F32)
    state[1:2, :] = jnp.zeros((1, total), F32)

    def visit(j, masked):
        slot = j - lo
        for t in range(total // tile):
            cols = slice(t * tile, (t + 1) * tile)
            q_t = q_all[cols, :]
            peak = state[0:1, cols]
            for half in range(2):
                cut = slice(half * rows, (half + 1) * rows)
                s = nt(k_win[j, cut, :], q_t) * unit
                if masked:
                    key_pos = key_iota + (base + (j * 2 + (core if half == 0 else 1 - core)) * rows)
                    s = jnp.where((key_pos >= firsts) & (key_pos <= lasts), s, NEG_FILL)
                peak = jnp.maximum(peak, jnp.max(s, axis=0, keepdims=True))
                raw[cut, cols] = s
            factors[slot, 0:1, cols] = peak
        for t in range(total // tile):
            cols = slice(t * tile, (t + 1) * tile)
            old, peak = state[0:1, cols], factors[slot, 0:1, cols]
            seen = state[1:2, cols] * jnp.exp2(old - peak)
            for half in range(2):
                cut = slice(half * rows, (half + 1) * rows)
                p = jnp.exp2(raw[cut, cols] - peak)
                p_all[slot, cut, cols] = p
                seen = seen + jnp.sum(p, axis=0, keepdims=True)
            state[0:1, cols] = peak
            state[1:2, cols] = seen
        pltpu.make_async_copy(p_all.at[slot], p_out.at[slot], sems.at[slot]).start()

    def plain(j, carry):
        visit(j, False)
        return carry

    def edges(i, carry):
        visit(jnp.where(lo + i < edge, lo + i, here), True)
        return carry

    lax.fori_loop(0, edge - lo + 1, edges, 0)
    lax.fori_loop(edge, here, plain, 0)
    state[1:2, :] = 1.0 / state[1:2, :]

    def second(j, carry):
        slot = j - lo
        dv = jnp.zeros((2 * rows, hd), F32)
        for g in range(total // group):
            for t in range(g * group // tile, (g + 1) * group // tile):
                cols = slice(t * tile, (t + 1) * tile)
                factor = jnp.exp2(factors[slot, 0:1, cols] - state[0:1, cols]) * state[1:2, cols]
                factors[slot, 0:1, cols] = factor
                for half in range(2):
                    cut = slice(half * rows, (half + 1) * rows)
                    low[cut, cols] = (p_all[slot, cut, cols] * factor).astype(BF)
            span = slice(g * group, (g + 1) * group)
            dv = dv + nn(low[:, span], do_all[span, :])
        at = out_index(j, z, zs)
        dv_own[at] = dv[:rows]
        dv_other[at] = dv[rows:]
        return carry

    lax.fori_loop(lo, here + 1, second, 0)

    def clear(j, carry):
        at = out_index(j, z, zs)
        dv_own[at] = jnp.zeros((rows, hd), F32)
        dv_other[at] = jnp.zeros((rows, hd), F32)
        return carry

    lax.fori_loop(z, lo, clear, 0)

    def finish(j, carry):
        slot = j - lo
        pltpu.make_async_copy(p_all.at[slot], p_out.at[slot], sems.at[slot]).wait()
        return carry

    lax.fori_loop(lo, here + 1, finish, 0)


def score_kernel(
    place_ref,
    info_ref,
    q_ref,
    do_ref,
    o_ref,
    k_own,
    k_other,
    far_own,
    far_other,
    v_own,
    v_other,
    far_v_own,
    far_v_other,
    factors,
    owner_ref,
    p_in,
    packed_ref,
    dk_own,
    dk_other,
    q_all,
    do_all,
    k_win,
    v_win,
    p_all,
    low,
    delta,
    dq_sum,
    sems,
    *,
    zs,
    scale,
    tile,
    group,
    block,
):
    rows, width = q_ref.shape
    hd = q_all.shape[1]
    total = q_all.shape[0]
    z = place_ref[1]
    here = 2 * zs + z
    lo = info_ref[0]

    def copy_in(slot):
        return pltpu.make_async_copy(p_in.at[slot], p_all.at[slot], sems.at[slot])

    def begin(j, carry):
        copy_in(j - lo).start()
        return carry

    lax.fori_loop(lo, here + 1, begin, 0)
    stack_heads(q_all, q_ref)
    stack_heads(do_all, do_ref)
    fill_window(k_win, k_own, k_other, far_own[:rows, :], far_other[:rows, :], z, zs)
    fill_window(v_win, v_own, v_other, far_v_own[...], far_v_other[...], z, zs)
    for n in range(width // hd):
        cols = slice(n * hd, (n + 1) * hd)
        prod = do_ref[:, cols].astype(F32) * o_ref[:, cols].astype(F32)
        delta[0:1, n * rows : (n + 1) * rows] = jnp.sum(prod.T, axis=0, keepdims=True)
    dq_sum[...] = jnp.zeros_like(dq_sum)

    def clear(j, carry):
        at = relative_index(j, z, zs)
        dk_own[at] = jnp.zeros((rows, hd), F32)
        dk_other[at] = jnp.zeros((rows, hd), F32)
        return carry

    lax.fori_loop(z, lo, clear, 0)

    def visit(j, carry):
        slot = j - lo
        copy_in(slot).wait()
        keys_t = k_win[j].T
        dk = jnp.zeros((2 * rows, hd), F32)
        for g in range(total // group):
            for t in range(g * group // tile, (g + 1) * group // tile):
                cols = slice(t * tile, (t + 1) * tile)
                do_t = do_all[cols, :]
                for half in range(2):
                    cut = slice(half * rows, (half + 1) * rows)
                    dprob = nt(v_win[j, cut, :], do_t)
                    probs = p_all[slot, cut, cols] * factors[slot, 0:1, cols]
                    low[cut, cols] = (probs * (dprob - delta[0:1, cols]) * scale).astype(BF)
            span = slice(g * group, (g + 1) * group)
            dk = dk + nn(low[:, span], q_all[span, :])
            dq_sum[:, span] += nn(keys_t, low[:, span])
        at = relative_index(j, z, zs)
        dk_own[at] = dk[:rows]
        dk_other[at] = dk[rows:]
        return carry

    lax.fori_loop(lo, here + 1, visit, 0)
    half_width = width // 2
    half_heads = half_width // hd
    spots = packed_ref.shape[0]
    row = lax.broadcasted_iota(jnp.int32, (spots, rows), 0)
    token = lax.broadcasted_iota(jnp.int32, (spots, rows), 1)
    goes = (row // (2 * block) == owner_ref[...]) & (row % block == token % block)
    packed = jnp.zeros((spots, half_width), F32)
    for h in range(2):
        here_half = goes & (row // block % 2 == h)
        turned = [
            dq_sum[:, n * rows : (n + 1) * rows].T.astype(BF)
            for n in range(h * half_heads, (h + 1) * half_heads)
        ]
        packed = packed + nn(here_half.astype(F32).astype(BF), jnp.concatenate(turned, axis=1))
    packed_ref[...] = packed.astype(BF)


def swap(value):
    return lax.ppermute(value, "core", [(0, 1), (1, 0)])


def first_payload_kernel(keys_ref, values_ref, doc_ref, owner_ref, out_ref, notes, *, xs):
    part, groups, hd = keys_ref.shape
    extra, width = notes.shape
    per_device = owner_ref.shape[1]
    row = lax.broadcasted_iota(jnp.int32, (extra, doc_ref.shape[1]), 0)
    earlier = jnp.sum((doc_ref[...] < row).astype(F32), axis=1, keepdims=True)
    notes[...] = jnp.broadcast_to(earlier, (extra, width))
    notes[COUNTS:, :per_device] = jnp.broadcast_to(
        owner_ref[...].astype(F32), (extra - COUNTS, per_device)
    )
    low = notes[...].astype(BF)
    for g in range(groups):
        k, v = keys_ref[:, g, :], values_ref[:, g, :]
        for at in range(g * xs, (g + 1) * xs):
            out_ref[at, :part, :hd] = k
            out_ref[at, :part, hd:] = v
            out_ref[at, part:, :] = low


def pick_kernel(place_ref, k_own, k_other, pick_ref, *, block, per_device, xs):
    zs, _, tall, hd = k_own.shape
    extra = COUNTS + xs
    first = tall - extra
    rows, spots = pick_ref.shape[1:]
    core, me = place_ref[2], place_ref[5]
    slot = lax.broadcasted_iota(jnp.int32, (rows, hd), 0) // block
    to_rows = (slot == lax.broadcasted_iota(jnp.int32, (rows, hd), 1)).astype(F32).astype(BF)
    held = lax.broadcasted_iota(jnp.int32, (zs * extra, hd), 0) % extra >= COUNTS
    held = held & (lax.broadcasted_iota(jnp.int32, (zs * extra, hd), 1) < per_device)
    line = lax.broadcasted_iota(jnp.int32, (zs * extra, spots), 0)
    peer = lax.broadcasted_iota(jnp.int32, (zs * extra, spots), 1) // (2 * block)
    pick = jnp.zeros((rows, spots), F32)
    for notes, c in ((k_own, core), (k_other, 1 - core)):
        owners = jnp.concatenate([notes[zz, 0, first:, :].astype(F32) for zz in range(zs)], axis=0)
        hit = (held & (owners == me.astype(F32))).astype(F32).astype(BF)
        source = ((line % extra - COUNTS) * zs + line // extra) * 2 + c
        to_spots = ((source == peer) & (line % extra >= COUNTS)).astype(F32).astype(BF)
        pick = pick + nn(nt(to_rows, hit).astype(BF), to_spots)
    row = lax.broadcasted_iota(jnp.int32, (rows, spots), 0)
    spot = lax.broadcasted_iota(jnp.int32, (rows, spots), 1)
    same = spot % block == row % block
    for h in range(2):
        pick_ref[h] = jnp.where(same & (spot // block % 2 == h), pick, 0.0).astype(BF)


def placement_kernel(pick_ref, arrived_ref, out_ref):
    half_width = arrived_ref.shape[1]
    for h in range(2):
        out_ref[:, h * half_width : (h + 1) * half_width] = nn(
            pick_ref[h], arrived_ref[...]
        ).astype(BF)


def along_x(parts, xs):
    mine, near, far = parts
    from_next = lax.ppermute(near, "x", [(i, i - 1) for i in range(1, xs)])
    from_last = lax.ppermute(far, "x", [(i, i - 2) for i in range(2, xs)])
    return (mine + from_next + from_last).astype(BF)


def reduce_at_once(own, other, zs, z):
    rows, hd = own.shape[1:]
    swapped = swap(other)
    sent = (own[: 2 * zs] + swapped[: 2 * zs]).astype(BF).reshape(zs, 2, rows, hd)
    came = lax.all_to_all(sent, "z", split_axis=0, concat_axis=0, tiled=True)
    came = came.astype(F32)
    later = (jnp.arange(zs) >= z)[:, None, None]
    mine = jnp.sum(jnp.where(later, came[:, 1], 0.0), axis=0)
    near = jnp.sum(came[:, 0], axis=0)
    far = jnp.sum(jnp.where(later, 0.0, came[:, 1]), axis=0) + own[2 * zs] + swapped[2 * zs]
    return mine, near, far


def reduce_by_shifts(own, other, zs, z):
    swapped = swap(other)
    came = []
    for k in range(1, zs):
        sent = (own[2 * k : 2 * k + 2] + swapped[2 * k : 2 * k + 2]).astype(BF)
        came.append(lax.ppermute(sent, "z", [(i, (i + k) % zs) for i in range(zs)]))
    mine = own[1] + swapped[1]
    near = own[0] + swapped[0]
    far = own[2 * zs] + swapped[2 * zs]
    for k, got in enumerate(came, 1):
        near = near + got[0].astype(F32)
        mine = mine + jnp.where(z < k, got[1].astype(F32), 0.0)
        far = far + jnp.where(z < k, 0.0, got[1].astype(F32))
    return mine, near, far


def program(queries, keys, values, outputs, grad_out, doc_ids, owner):
    hd = keys.shape[2]
    scale = hd**-0.5
    rows, _, width = queries.shape
    total = rows * (width // hd)
    tile = min(256, total)
    group = min(512, total)
    xs, zs = lax.axis_size("x"), lax.axis_size("z")
    x, z, core = lax.axis_index("x"), lax.axis_index("z"), lax.axis_index("core")
    peers = xs * zs * 2
    per_device = owner.shape[0]
    block_len = rows // per_device
    part = keys.shape[0]
    chips = 2 * zs + 1

    extra = COUNTS + xs
    vmem = pl.BlockSpec(memory_space=pltpu.VMEM)
    smem = pl.BlockSpec(memory_space=pltpu.SMEM)
    anywhere = pl.BlockSpec(memory_space=pl.ANY)
    mixed = pl.pallas_call(
        functools.partial(first_payload_kernel, xs=xs),
        in_specs=[vmem] * 4,
        out_specs=vmem,
        out_shape=jax.ShapeDtypeStruct((4 * xs, part + extra, 2 * hd), BF),
        scratch_shapes=[pltpu.VMEM((extra, 2 * hd), F32)],
        name="first_payload",
    )(keys, values, doc_ids[None], owner[None])
    mixed = lax.all_to_all(
        mixed,
        ("dp", "head", "x"),
        split_axis=0,
        concat_axis=0,
        tiled=True,
    ).reshape(2, 2, xs, part + extra, 2 * hd)

    def piece(back):
        got = lax.dynamic_index_in_dim(mixed, lax.rem(x - back + xs, xs), 2, keepdims=False)
        tokens = jnp.transpose(got[:, :, :part], (1, 0, 2, 3)).reshape(rows, 2 * hd)
        return jnp.concatenate([tokens, got[0, 0, part:]], axis=0)

    last, near, far = piece(0), piece(1), piece(2)
    far_other = swap(far)

    def along_z(a, b, c):
        ahead = (jnp.arange(zs) >= z)[:, None, None]
        chosen = jnp.where(ahead, a[None], c[None])
        pair = jnp.stack([jnp.broadcast_to(b[None], chosen.shape), chosen], axis=1)
        return lax.all_to_all(pair, "z", split_axis=0, concat_axis=0, tiled=True)

    held = mixed[0, 0, :, part + COUNTS, :hd]
    near_keys = jnp.concatenate([near[: rows + COUNTS, :hd], held], axis=0)
    k_own = along_z(last[:, :hd], near_keys, far[:, :hd])
    k_other = swap(k_own)
    v_own = along_z(last[:rows, hd:], near[:rows, hd:], far[:rows, hd:])

    base = (x - 2) * (zs * 2 * rows)
    me = (x * zs + z) * 2 + core
    place = jnp.stack([x, z, core, base, jnp.maximum(base + z * 2 * rows, 0), me]).astype(jnp.int32)
    q = queries.reshape(rows, width)
    do = grad_out.reshape(rows, width)
    o = outputs.reshape(rows, width)
    grad_shape = jax.ShapeDtypeStruct((chips, rows, hd), F32)
    params = pltpu.CompilerParams(vmem_limit_bytes=VMEM_BYTES)
    dv_own, dv_other, probs, info, factors = pl.pallas_call(
        functools.partial(softmax_kernel, zs=zs, scale=scale, tile=tile, group=group),
        in_specs=[smem] + [vmem] * 7,
        out_specs=[vmem, vmem, anywhere, smem, vmem],
        out_shape=[
            grad_shape,
            grad_shape,
            jax.ShapeDtypeStruct((chips, 2 * rows, total), F32),
            jax.ShapeDtypeStruct((1,), jnp.int32),
            jax.ShapeDtypeStruct((chips, 8, total), F32),
        ],
        scratch_shapes=[
            pltpu.VMEM((total, hd), BF),
            pltpu.VMEM((total, hd), BF),
            pltpu.VMEM((3 * zs, 2 * rows, hd), BF),
            pltpu.VMEM((chips, 2 * rows, total), F32),
            pltpu.VMEM((2 * rows, total), F32),
            pltpu.VMEM((2 * rows, total), BF),
            pltpu.VMEM((8, total), F32),
            pltpu.SemaphoreType.DMA((chips,)),
        ],
        compiler_params=params,
        cost_estimate=pl.CostEstimate(
            flops=12_000_000_000, bytes_accessed=20_000_000, transcendentals=4_000_000
        ),
        name="softmax_and_value_gradient",
    )(
        place,
        q,
        do,
        doc_ids.reshape(1, rows),
        k_own,
        k_other,
        far[:, :hd],
        far_other[:, :hd],
    )
    v_other = swap(v_own)
    parts_v = reduce_at_once(dv_own, dv_other, zs, z)
    packed, dk_own, dk_other = pl.pallas_call(
        functools.partial(
            score_kernel, zs=zs, scale=scale, tile=tile, group=group, block=block_len
        ),
        in_specs=[smem, smem] + [vmem] * 13 + [anywhere],
        out_specs=[vmem] * 3,
        out_shape=[
            jax.ShapeDtypeStruct((peers * 2 * block_len, width // 2), BF),
            grad_shape,
            grad_shape,
        ],
        scratch_shapes=[
            pltpu.VMEM((total, hd), BF),
            pltpu.VMEM((total, hd), BF),
            pltpu.VMEM((3 * zs, 2 * rows, hd), BF),
            pltpu.VMEM((3 * zs, 2 * rows, hd), BF),
            pltpu.VMEM((chips, 2 * rows, total), F32),
            pltpu.VMEM((2 * rows, total), BF),
            pltpu.VMEM((8, total), F32),
            pltpu.VMEM((hd, total), F32),
            pltpu.SemaphoreType.DMA((chips,)),
        ],
        compiler_params=params,
        cost_estimate=pl.CostEstimate(
            flops=12_000_000_000, bytes_accessed=20_000_000, transcendentals=0
        ),
        name="score_gradient",
    )(
        place,
        info,
        q,
        do,
        o,
        k_own,
        k_other,
        far[:, :hd],
        far_other[:, :hd],
        v_own,
        v_other,
        far[:rows, hd:],
        far_other[:rows, hd:],
        factors,
        jnp.repeat(owner, block_len)[None],
        probs,
    )
    parts_k = reduce_by_shifts(dk_own, dk_other, zs, z)
    grads = along_x([jnp.concatenate(pair, axis=1) for pair in zip(parts_k, parts_v)], xs)
    grad_k, grad_v = grads[:, None, :hd], grads[:, None, hd:]

    pick = pl.pallas_call(
        functools.partial(pick_kernel, block=block_len, per_device=per_device, xs=xs),
        in_specs=[smem, vmem, vmem],
        out_specs=vmem,
        out_shape=jax.ShapeDtypeStruct((2, rows, peers * 2 * block_len), BF),
        cost_estimate=pl.CostEstimate(flops=100_000_000, bytes_accessed=1_000_000, transcendentals=0),
        name="placement_choice",
    )(place, k_own, k_other)
    arrived = lax.all_to_all(
        packed.reshape(peers, 2 * block_len, width // 2),
        ("x", "z", "core"),
        split_axis=0,
        concat_axis=0,
        tiled=True,
    )
    placed = pl.pallas_call(
        placement_kernel,
        in_specs=[vmem, vmem],
        out_specs=vmem,
        out_shape=jax.ShapeDtypeStruct((rows, width), BF),
        compiler_params=params,
        name="query_gradient_placement",
    )(pick, arrived.reshape(packed.shape))
    return (placed.reshape(rows, 1, width), grad_k, grad_v)


def solution(mesh):
    sizes = mesh.shape
    dp, ctx, head = sizes["dp"], sizes["ctx"], sizes["head"]
    xs = 4
    fine = Mesh(
        mesh.devices.reshape(dp, xs, ctx // (2 * xs), 2, head), ("dp", "x", "z", "core", "head")
    )
    ctx_axes = ("x", "z", "core")
    heads = P(ctx_axes, ("dp", "head"), None)
    tokens = P(ctx_axes + ("head", "dp"), None, None)
    return jax.shard_map(
        program,
        mesh=fine,
        in_specs=(heads, tokens, tokens, heads, heads, P(ctx_axes), P(ctx_axes)),
        out_specs=(heads, heads, heads),
        check_vma=False,
    )
```

```python
import functools
import math

import jax
import jax.numpy as jnp
from jax import lax
from jax.experimental import pallas as pl
from jax.experimental.pallas import tpu as pltpu
from jax.sharding import Mesh, PartitionSpec as P


NEG_FILL = -1e30
VMEM_BYTES = 60 * 1024 * 1024
BF = jnp.bfloat16
F32 = jnp.float32
COUNTS = 4


def nt(a, b):
    return lax.dot_general(a, b, (((1,), (1,)), ((), ())), preferred_element_type=F32)


def nn(a, b):
    return lax.dot_general(a, b, (((1,), (0,)), ((), ())), preferred_element_type=F32)


def stack_heads(dst, src):
    rows, width = src.shape
    hd = dst.shape[1]
    for n in range(width // hd):
        dst[n * rows : (n + 1) * rows, :] = src[:, n * hd : (n + 1) * hd]


def fill_window(win, own, other, far_own, far_other, z, zs, cols, rows):
    hd = win.shape[1]

    def at(j, half):
        start = (j + 1) * 2 * rows + half * rows
        return pl.ds(start if isinstance(start, int) else pl.multiple_of(start, rows), rows)

    for half, near, far in ((0, own, far_own), (1, other, far_other)):
        for zz in range(zs):
            win[at(zs + zz, half), :] = near[zz, 0, :rows, :]
            win[at(jnp.where(zz > z, zz, 2 * zs + zz), half), :] = near[zz, 1, :rows, :]
        win[at(z, half), :] = far[:rows, cols]
        win[at(z - 1, half), :] = jnp.zeros((rows, hd), BF)


def out_index(j, z, zs):
    zz = lax.rem(j, zs)
    middle = (j >= zs) & (j < 2 * zs)
    return jnp.where(middle, 2 * zz, jnp.where(j == z, 2 * zs, 2 * zz + 1))


def relative_index(j, z, zs):
    zz = lax.rem(lax.rem(j, zs) + zs - z, zs)
    middle = (j >= zs) & (j < 2 * zs)
    return jnp.where(middle, 2 * zz, jnp.where(j == z, 2 * zs, 2 * zz + 1))


def store_pair(j, value, own, other, z, index):
    rows = own.shape[1]

    @pl.when(j >= z)
    def _():
        own[index(j)] = value[:rows]
        other[index(j)] = value[rows : 2 * rows]

    own[index(j + 1)] = value[2 * rows : 3 * rows]
    other[index(j + 1)] = value[3 * rows :]


def softmax_kernel(
    place_ref,
    q_ref,
    do_ref,
    doc_ref,
    k_own,
    k_other,
    far_own,
    far_other,
    dv_own,
    dv_other,
    p_out,
    info_ref,
    factors,
    q_all,
    do_all,
    k_win,
    p_all,
    raw,
    low,
    state,
    sems,
    *,
    zs,
    scale,
    tile,
    group,
):
    rows, _ = q_ref.shape
    hd = q_all.shape[1]
    total = q_all.shape[0]
    x, z, core = place_ref[0], place_ref[1], place_ref[2]
    base, reach = place_ref[3], place_ref[4]
    here = 2 * zs + z
    unit = scale * math.log2(math.e)

    stack_heads(q_all, q_ref)
    stack_heads(do_all, do_ref)
    fill_window(k_win, k_own, k_other, far_own, far_other, z, zs, slice(0, hd), rows)

    near_ok = (x >= 1).astype(F32)
    far_ok = (x >= 2).astype(F32)
    counts = (
        far_own[rows : rows + COUNTS, :hd].astype(F32)
        + far_other[rows : rows + COUNTS, :hd].astype(F32)
    ) * far_ok
    for zz in range(zs):
        both = k_own[zz, 0, rows : rows + COUNTS, :].astype(F32) + k_other[
            zz, 0, rows : rows + COUNTS, :
        ].astype(F32)
        counts = counts + both * near_ok
        both = k_own[zz, 1, rows : rows + COUNTS, :].astype(F32) + k_other[
            zz, 1, rows : rows + COUNTS, :
        ].astype(F32)
        counts = counts + both * jnp.where(zz > z, far_ok, 1.0)
    doc = doc_ref[...]
    first_row = jnp.zeros((1, rows), F32)
    for d in range(1, COUNTS):
        first_row = jnp.where(doc == d, counts[d : d + 1, :rows], first_row)
    first_row = first_row.astype(jnp.int32) + reach
    lo = (jnp.min(first_row) - base) // (2 * rows)
    edge = jnp.minimum((jnp.max(first_row) - base) // (2 * rows) + 1, here)
    info_ref[0] = lo
    pairs = (here - lo + 2) // 2
    start = here + 1 - 2 * pairs
    inner = jnp.minimum((edge - start + 1) // 2, pairs - 1)
    q_pos = base + (here * 2 + core) * rows + lax.broadcasted_iota(jnp.int32, (1, rows), 1)
    firsts = jnp.concatenate([first_row] * (tile // rows), axis=1)
    lasts = jnp.concatenate([q_pos] * (tile // rows), axis=1)
    key_iota = lax.broadcasted_iota(jnp.int32, (rows, tile), 0)

    state[0:1, :] = jnp.full((1, total), NEG_FILL, F32)
    state[1:2, :] = jnp.zeros((1, total), F32)

    def pair_rows(i):
        return pl.ds(pl.multiple_of((start + 2 * i + 1) * 2 * rows, 2 * rows), 4 * rows)

    def visit(i, masked):
        keys = k_win[pair_rows(i), :]
        for t in range(total // tile):
            cols = slice(t * tile, (t + 1) * tile)
            q_t = q_all[cols, :]
            peak = state[0:1, cols]
            for c in range(4):
                cut = slice(c * rows, (c + 1) * rows)
                s = nt(keys[cut], q_t) * unit
                if masked:
                    chip = start + 2 * i + c // 2
                    key_pos = key_iota + (base + (chip * 2 + (core if c % 2 == 0 else 1 - core)) * rows)
                    s = jnp.where((key_pos >= firsts) & (key_pos <= lasts), s, NEG_FILL)
                peak = jnp.maximum(peak, jnp.max(s, axis=0, keepdims=True))
                raw[cut, cols] = s
            factors[i, 0:1, cols] = peak
        for t in range(total // tile):
            cols = slice(t * tile, (t + 1) * tile)
            old, peak = state[0:1, cols], factors[i, 0:1, cols]
            seen = state[1:2, cols] * jnp.exp2(old - peak)
            for c in range(4):
                cut = slice(c * rows, (c + 1) * rows)
                p = jnp.exp2(raw[cut, cols] - peak)
                p_all[i, cut, cols] = p
                seen = seen + jnp.sum(p, axis=0, keepdims=True)
            state[0:1, cols] = peak
            state[1:2, cols] = seen
        pltpu.make_async_copy(p_all.at[i], p_out.at[i], sems.at[i]).start()

    def plain(i, carry):
        visit(i, False)
        return carry

    def edges(i, carry):
        visit(jnp.where(i < inner, i, pairs - 1), True)
        return carry

    lax.fori_loop(0, inner + 1, edges, 0)
    lax.fori_loop(inner, pairs - 1, plain, 0)
    state[1:2, :] = 1.0 / state[1:2, :]

    def second(i, carry):
        dv = None
        for g in range(total // group):
            for t in range(g * group // tile, (g + 1) * group // tile):
                cols = slice(t * tile, (t + 1) * tile)
                factor = jnp.exp2(factors[i, 0:1, cols] - state[0:1, cols]) * state[1:2, cols]
                factors[i, 0:1, cols] = factor
                for c in range(4):
                    cut = slice(c * rows, (c + 1) * rows)
                    low[cut, cols] = (p_all[i, cut, cols] * factor).astype(BF)
            span = slice(g * group, (g + 1) * group)
            more = nn(low[:, span], do_all[span, :])
            dv = more if dv is None else dv + more
        store_pair(start + 2 * i, dv, dv_own, dv_other, z, lambda j: out_index(j, z, zs))
        return carry

    lax.fori_loop(0, pairs, second, 0)

    def clear(j, carry):
        at = out_index(j, z, zs)
        dv_own[at] = jnp.zeros((rows, hd), F32)
        dv_other[at] = jnp.zeros((rows, hd), F32)
        return carry

    lax.fori_loop(z, lo, clear, 0)

    def finish(i, carry):
        pltpu.make_async_copy(p_all.at[i], p_out.at[i], sems.at[i]).wait()
        return carry

    lax.fori_loop(0, pairs, finish, 0)


def score_kernel(
    place_ref,
    info_ref,
    q_ref,
    do_ref,
    o_ref,
    k_own,
    k_other,
    far_own,
    far_other,
    v_own,
    v_other,
    factors,
    owner_ref,
    p_in,
    packed_ref,
    dk_own,
    dk_other,
    q_all,
    do_all,
    k_win,
    v_win,
    p_all,
    low,
    delta,
    dq_sum,
    sems,
    *,
    zs,
    scale,
    tile,
    group,
    block,
):
    rows, width = q_ref.shape
    hd = q_all.shape[1]
    total = q_all.shape[0]
    z = place_ref[1]
    here = 2 * zs + z
    lo = info_ref[0]

    def copy_in(slot):
        return pltpu.make_async_copy(p_in.at[slot], p_all.at[slot], sems.at[slot])

    pairs = (here - lo + 2) // 2
    start = here + 1 - 2 * pairs

    def begin(i, carry):
        copy_in(i).start()
        return carry

    lax.fori_loop(0, pairs, begin, 0)
    stack_heads(q_all, q_ref)
    stack_heads(do_all, do_ref)
    fill_window(k_win, k_own, k_other, far_own, far_other, z, zs, slice(0, hd), rows)
    fill_window(v_win, v_own, v_other, far_own, far_other, z, zs, slice(hd, 2 * hd), rows)
    for n in range(width // hd):
        cols = slice(n * hd, (n + 1) * hd)
        prod = do_ref[:, cols].astype(F32) * o_ref[:, cols].astype(F32)
        delta[0:1, n * rows : (n + 1) * rows] = jnp.sum(prod.T, axis=0, keepdims=True)
    dq_sum[...] = jnp.zeros_like(dq_sum)

    def clear(j, carry):
        at = relative_index(j, z, zs)
        dk_own[at] = jnp.zeros((rows, hd), F32)
        dk_other[at] = jnp.zeros((rows, hd), F32)
        return carry

    lax.fori_loop(z, lo, clear, 0)

    def visit(i, carry):
        copy_in(i).wait()
        window = pl.ds(pl.multiple_of((start + 2 * i + 1) * 2 * rows, 2 * rows), 4 * rows)
        keys_t = k_win[window, :].T
        values = v_win[window, :]
        dk = None
        for g in range(total // group):
            for t in range(g * group // tile, (g + 1) * group // tile):
                cols = slice(t * tile, (t + 1) * tile)
                do_t = do_all[cols, :]
                for c in range(4):
                    cut = slice(c * rows, (c + 1) * rows)
                    dprob = nt(values[cut], do_t)
                    probs = p_all[i, cut, cols] * factors[i, 0:1, cols]
                    low[cut, cols] = (probs * (dprob - delta[0:1, cols]) * scale).astype(BF)
            span = slice(g * group, (g + 1) * group)
            more = nn(low[:, span], q_all[span, :])
            dk = more if dk is None else dk + more
            dq_sum[:, span] += nn(keys_t, low[:, span])
        store_pair(start + 2 * i, dk, dk_own, dk_other, z, lambda j: relative_index(j, z, zs))
        return carry

    lax.fori_loop(0, pairs, visit, 0)
    half_width = width // 2
    half_heads = half_width // hd
    spots = packed_ref.shape[0]
    row = lax.broadcasted_iota(jnp.int32, (spots, rows), 0)
    token = lax.broadcasted_iota(jnp.int32, (spots, rows), 1)
    slots = owner_ref.shape[1]
    spread = lax.broadcasted_iota(jnp.int32, (slots, rows), 1) // block
    spread = spread == lax.broadcasted_iota(jnp.int32, (slots, rows), 0)
    owners = jnp.broadcast_to(owner_ref[...].astype(F32).astype(BF), (8, slots))
    owners = nn(owners, spread.astype(F32).astype(BF))[0:1]
    goes = ((row // (2 * block)).astype(F32) == owners) & (row % block == token % block)
    packed = jnp.zeros((spots, half_width), F32)
    for h in range(2):
        here_half = goes & (row // block % 2 == h)
        turned = [
            dq_sum[:, n * rows : (n + 1) * rows].T.astype(BF)
            for n in range(h * half_heads, (h + 1) * half_heads)
        ]
        packed = packed + nn(here_half.astype(F32).astype(BF), jnp.concatenate(turned, axis=1))
    packed_ref[...] = packed.astype(BF)


def swap(value):
    return lax.ppermute(value, "core", [(0, 1), (1, 0)])


def first_payload_kernel(keys_ref, values_ref, doc_ref, owner_ref, out_ref, notes, *, xs):
    part, groups, hd = keys_ref.shape
    extra, width = notes.shape
    per_device = owner_ref.shape[1]
    row = lax.broadcasted_iota(jnp.int32, (extra, doc_ref.shape[1]), 0)
    earlier = jnp.sum((doc_ref[...] < row).astype(F32), axis=1, keepdims=True)
    notes[...] = jnp.broadcast_to(earlier, (extra, width))
    notes[COUNTS:, :per_device] = jnp.broadcast_to(
        owner_ref[...].astype(F32), (extra - COUNTS, per_device)
    )
    low = notes[...].astype(BF)
    for g in range(groups):
        k, v = keys_ref[:, g, :], values_ref[:, g, :]
        for at in range(g * xs, (g + 1) * xs):
            out_ref[at, :part, :hd] = k
            out_ref[at, :part, hd:] = v
            out_ref[at, part:, :] = low


def pick_kernel(place_ref, k_own, k_other, pick_ref, *, block, per_device, xs):
    zs, _, tall, hd = k_own.shape
    extra = COUNTS + xs
    first = tall - extra
    rows, spots = pick_ref.shape[1:]
    core, me = place_ref[2], place_ref[5]
    slot = lax.broadcasted_iota(jnp.int32, (rows, hd), 0) // block
    to_rows = (slot == lax.broadcasted_iota(jnp.int32, (rows, hd), 1)).astype(F32).astype(BF)
    held = lax.broadcasted_iota(jnp.int32, (zs * extra, hd), 0) % extra >= COUNTS
    held = held & (lax.broadcasted_iota(jnp.int32, (zs * extra, hd), 1) < per_device)
    line = lax.broadcasted_iota(jnp.int32, (zs * extra, spots), 0)
    peer = lax.broadcasted_iota(jnp.int32, (zs * extra, spots), 1) // (2 * block)
    pick = jnp.zeros((rows, spots), F32)
    for notes, c in ((k_own, core), (k_other, 1 - core)):
        owners = jnp.concatenate([notes[zz, 0, first:, :].astype(F32) for zz in range(zs)], axis=0)
        hit = (held & (owners == me.astype(F32))).astype(F32).astype(BF)
        source = ((line % extra - COUNTS) * zs + line // extra) * 2 + c
        to_spots = ((source == peer) & (line % extra >= COUNTS)).astype(F32).astype(BF)
        pick = pick + nn(nt(to_rows, hit).astype(BF), to_spots)
    row = lax.broadcasted_iota(jnp.int32, (rows, spots), 0)
    spot = lax.broadcasted_iota(jnp.int32, (rows, spots), 1)
    same = spot % block == row % block
    for h in range(2):
        pick_ref[h] = jnp.where(same & (spot // block % 2 == h), pick, 0.0).astype(BF)


def placement_kernel(pick_ref, arrived_ref, out_ref):
    half_width = arrived_ref.shape[1]
    for h in range(2):
        out_ref[:, h * half_width : (h + 1) * half_width] = nn(
            pick_ref[h], arrived_ref[...]
        ).astype(BF)


def along_x(parts, xs):
    mine, near, far = parts
    from_next = lax.ppermute(near, "x", [(i, i - 1) for i in range(1, xs)])
    from_last = lax.ppermute(far, "x", [(i, i - 2) for i in range(2, xs)])
    return (mine + from_next + from_last).astype(BF)


def reduce_at_once(own, other, zs, z):
    rows, hd = own.shape[1:]
    swapped = swap(other)
    sent = (own[: 2 * zs] + swapped[: 2 * zs]).astype(BF).reshape(zs, 2, rows, hd)
    came = lax.all_to_all(sent, "z", split_axis=0, concat_axis=0, tiled=True)
    came = came.astype(F32)
    later = (jnp.arange(zs) >= z)[:, None, None]
    mine = jnp.sum(jnp.where(later, came[:, 1], 0.0), axis=0)
    near = jnp.sum(came[:, 0], axis=0)
    far = jnp.sum(jnp.where(later, 0.0, came[:, 1]), axis=0) + own[2 * zs] + swapped[2 * zs]
    return mine, near, far


def reduce_by_shifts(own, other, zs, z):
    swapped = swap(other)
    came = []
    for k in range(1, zs):
        sent = (own[2 * k : 2 * k + 2] + swapped[2 * k : 2 * k + 2]).astype(BF)
        came.append(lax.ppermute(sent, "z", [(i, (i + k) % zs) for i in range(zs)]))
    mine = own[1] + swapped[1]
    near = own[0] + swapped[0]
    far = own[2 * zs] + swapped[2 * zs]
    for k, got in enumerate(came, 1):
        near = near + got[0].astype(F32)
        mine = mine + jnp.where(z < k, got[1].astype(F32), 0.0)
        far = far + jnp.where(z < k, 0.0, got[1].astype(F32))
    return mine, near, far, came[zs // 2]


def program(queries, keys, values, outputs, grad_out, doc_ids, owner):
    hd = keys.shape[2]
    scale = hd**-0.5
    rows, _, width = queries.shape
    total = rows * (width // hd)
    tile = min(256, total)
    group = min(1024, total)
    xs, zs = lax.axis_size("x"), lax.axis_size("z")
    x, z, core = lax.axis_index("x"), lax.axis_index("z"), lax.axis_index("core")
    peers = xs * zs * 2
    per_device = owner.shape[0]
    block_len = rows // per_device
    part = keys.shape[0]
    chips = 2 * zs + 1
    steps = zs + 1

    extra = COUNTS + xs
    vmem = pl.BlockSpec(memory_space=pltpu.VMEM)
    smem = pl.BlockSpec(memory_space=pltpu.SMEM)
    anywhere = pl.BlockSpec(memory_space=pl.ANY)
    mixed = pl.pallas_call(
        functools.partial(first_payload_kernel, xs=xs),
        in_specs=[vmem] * 4,
        out_specs=vmem,
        out_shape=jax.ShapeDtypeStruct((4 * xs, part + extra, 2 * hd), BF),
        scratch_shapes=[pltpu.VMEM((extra, 2 * hd), F32)],
        name="first_payload",
    )(keys, values, doc_ids[None], owner[None])
    mixed = lax.all_to_all(
        mixed,
        ("dp", "head", "x"),
        split_axis=0,
        concat_axis=0,
        tiled=True,
    ).reshape(2, 2, xs, part + extra, 2 * hd)

    def piece(back):
        got = lax.dynamic_index_in_dim(mixed, lax.rem(x - back + xs, xs), 2, keepdims=False)
        tokens = jnp.transpose(got[:, :, :part], (1, 0, 2, 3)).reshape(rows, 2 * hd)
        return jnp.concatenate([tokens, got[0, 0, part:]], axis=0)

    last, near, far = piece(0), piece(1), piece(2)
    far_other = swap(far)

    def along_z(a, b, c):
        ahead = (jnp.arange(zs) >= z)[:, None, None]
        chosen = jnp.where(ahead, a[None], c[None])
        pair = jnp.stack([jnp.broadcast_to(b[None], chosen.shape), chosen], axis=1)
        return lax.all_to_all(pair, "z", split_axis=0, concat_axis=0, tiled=True)

    held = mixed[0, 0, :, part + COUNTS, :hd]
    near_keys = jnp.concatenate([near[: rows + COUNTS, :hd], held], axis=0)
    k_own = along_z(last[:, :hd], near_keys, far[:, :hd])
    k_other = swap(k_own)
    v_own = along_z(last[:rows, hd:], near[:rows, hd:], far[:rows, hd:])

    base = (x - 2) * (zs * 2 * rows)
    me = (x * zs + z) * 2 + core
    place = jnp.stack([x, z, core, base, jnp.maximum(base + z * 2 * rows, 0), me]).astype(jnp.int32)
    q = queries.reshape(rows, width)
    do = grad_out.reshape(rows, width)
    o = outputs.reshape(rows, width)
    grad_shape = jax.ShapeDtypeStruct((chips, rows, hd), F32)
    params = pltpu.CompilerParams(vmem_limit_bytes=VMEM_BYTES)
    small = pltpu.CompilerParams(vmem_limit_bytes=8 * 1024 * 1024)
    dv_own, dv_other, probs, info, factors = pl.pallas_call(
        functools.partial(softmax_kernel, zs=zs, scale=scale, tile=tile, group=group),
        in_specs=[smem] + [vmem] * 7,
        out_specs=[vmem, vmem, anywhere, smem, vmem],
        out_shape=[
            grad_shape,
            grad_shape,
            jax.ShapeDtypeStruct((steps, 4 * rows, total), F32),
            jax.ShapeDtypeStruct((1,), jnp.int32),
            jax.ShapeDtypeStruct((steps, 8, total), F32),
        ],
        scratch_shapes=[
            pltpu.VMEM((total, hd), BF),
            pltpu.VMEM((total, hd), BF),
            pltpu.VMEM(((3 * zs + 1) * 2 * rows, hd), BF),
            pltpu.VMEM((steps, 4 * rows, total), F32),
            pltpu.VMEM((4 * rows, total), F32),
            pltpu.VMEM((4 * rows, total), BF),
            pltpu.VMEM((8, total), F32),
            pltpu.SemaphoreType.DMA((steps,)),
        ],
        compiler_params=params,
        cost_estimate=pl.CostEstimate(
            flops=12_000_000_000, bytes_accessed=20_000_000, transcendentals=4_000_000
        ),
        name="softmax_and_value_gradient",
    )(
        place,
        q,
        do,
        doc_ids.reshape(1, rows),
        k_own,
        k_other,
        far,
        far_other,
    )
    v_other = swap(v_own)
    parts_v = reduce_at_once(dv_own, dv_other, zs, z)
    packed, dk_own, dk_other = pl.pallas_call(
        functools.partial(
            score_kernel, zs=zs, scale=scale, tile=tile, group=group, block=block_len
        ),
        in_specs=[smem, smem] + [vmem] * 11 + [anywhere],
        out_specs=[vmem] * 3,
        out_shape=[
            jax.ShapeDtypeStruct((peers * 2 * block_len, width // 2), BF),
            grad_shape,
            grad_shape,
        ],
        scratch_shapes=[
            pltpu.VMEM((total, hd), BF),
            pltpu.VMEM((total, hd), BF),
            pltpu.VMEM(((3 * zs + 1) * 2 * rows, hd), BF),
            pltpu.VMEM(((3 * zs + 1) * 2 * rows, hd), BF),
            pltpu.VMEM((steps, 4 * rows, total), F32),
            pltpu.VMEM((4 * rows, total), BF),
            pltpu.VMEM((8, total), F32),
            pltpu.VMEM((hd, total), F32),
            pltpu.SemaphoreType.DMA((steps,)),
        ],
        compiler_params=params,
        cost_estimate=pl.CostEstimate(
            flops=12_000_000_000, bytes_accessed=20_000_000, transcendentals=0
        ),
        name="score_gradient",
    )(
        place,
        info,
        q,
        do,
        o,
        k_own,
        k_other,
        far,
        far_other,
        v_own,
        v_other,
        factors,
        owner[None],
        probs,
    )
    *parts_k, halfway = reduce_by_shifts(dk_own, dk_other, zs, z)
    grads = along_x([jnp.concatenate(pair, axis=1) for pair in zip(parts_k, parts_v)], xs)
    grad_k, grad_v = grads[:, None, :hd], grads[:, None, hd:]

    pick = pl.pallas_call(
        functools.partial(pick_kernel, block=block_len, per_device=per_device, xs=xs),
        in_specs=[smem, vmem, vmem],
        out_specs=vmem,
        out_shape=jax.ShapeDtypeStruct((2, rows, peers * 2 * block_len), BF),
        cost_estimate=pl.CostEstimate(flops=100_000_000, bytes_accessed=1_000_000, transcendentals=0),
        compiler_params=small,
        name="placement_choice",
    )(lax.optimization_barrier((place, halfway))[0], k_own, k_other)
    arrived = lax.all_to_all(
        packed.reshape(peers, 2 * block_len, width // 2),
        ("x", "z", "core"),
        split_axis=0,
        concat_axis=0,
        tiled=True,
    )
    placed = pl.pallas_call(
        placement_kernel,
        in_specs=[vmem, vmem],
        out_specs=vmem,
        out_shape=jax.ShapeDtypeStruct((rows, width), BF),
        compiler_params=small,
        name="query_gradient_placement",
    )(pick, arrived.reshape(packed.shape))
    return (placed.reshape(rows, 1, width), grad_k, grad_v)


def solution(mesh):
    sizes = mesh.shape
    dp, ctx, head = sizes["dp"], sizes["ctx"], sizes["head"]
    xs = 4
    fine = Mesh(
        mesh.devices.reshape(dp, xs, ctx // (2 * xs), 2, head), ("dp", "x", "z", "core", "head")
    )
    ctx_axes = ("x", "z", "core")
    heads = P(ctx_axes, ("dp", "head"), None)
    tokens = P(ctx_axes + ("head", "dp"), None, None)
    return jax.shard_map(
        program,
        mesh=fine,
        in_specs=(heads, tokens, tokens, heads, heads, P(ctx_axes), P(ctx_axes)),
        out_specs=(heads, heads, heads),
        check_vma=False,
    )
```

```python
import functools
import math

import jax
import jax.numpy as jnp
from jax import lax
from jax.experimental import pallas as pl
from jax.experimental.pallas import tpu as pltpu
from jax.sharding import Mesh, PartitionSpec as P


NEG_FILL = -1e30
VMEM_BYTES = 60 * 1024 * 1024
BF = jnp.bfloat16
F32 = jnp.float32
COUNTS = 4


def nt(a, b):
    return lax.dot_general(a, b, (((1,), (1,)), ((), ())), preferred_element_type=F32)


def nn(a, b):
    return lax.dot_general(a, b, (((1,), (0,)), ((), ())), preferred_element_type=F32)


def stack_heads(dst, src):
    rows, width = src.shape
    hd = dst.shape[1]
    for n in range(width // hd):
        dst[n * rows : (n + 1) * rows, :] = src[:, n * hd : (n + 1) * hd]


def fill_window(win, own, other, far_own, far_other, z, zs, cols, rows):
    hd = win.shape[1]

    def at(j, half):
        start = (j + 1) * 2 * rows + half * rows
        return pl.ds(start if isinstance(start, int) else pl.multiple_of(start, rows), rows)

    for half, near, far in ((0, own, far_own), (1, other, far_other)):
        for zz in range(zs):
            win[at(zs + zz, half), :] = near[zz, 0, :rows, :]
            win[at(jnp.where(zz > z, zz, 2 * zs + zz), half), :] = near[zz, 1, :rows, :]
        win[at(z, half), :] = far[:rows, cols]
        win[at(z - 1, half), :] = jnp.zeros((rows, hd), BF)


def out_index(j, z, zs):
    zz = lax.rem(j, zs)
    middle = (j >= zs) & (j < 2 * zs)
    return jnp.where(middle, 2 * zz, jnp.where(j == z, 2 * zs, 2 * zz + 1))


def relative_index(j, z, zs):
    zz = lax.rem(lax.rem(j, zs) + zs - z, zs)
    middle = (j >= zs) & (j < 2 * zs)
    return jnp.where(middle, 2 * zz, jnp.where(j == z, 2 * zs, 2 * zz + 1))


def store_pair(j, value, own, other, z, index):
    rows = own.shape[1]

    @pl.when(j >= z)
    def _():
        own[index(j)] = value[:rows]
        other[index(j)] = value[rows : 2 * rows]

    own[index(j + 1)] = value[2 * rows : 3 * rows]
    other[index(j + 1)] = value[3 * rows :]


def softmax_kernel(
    place_ref,
    q_ref,
    do_ref,
    doc_ref,
    k_own,
    k_other,
    far_own,
    far_other,
    dv_own,
    dv_other,
    p_out,
    info_ref,
    factors,
    q_all,
    do_all,
    k_win,
    p_all,
    raw,
    low,
    state,
    sems,
    *,
    zs,
    scale,
    tile,
    group,
):
    rows, _ = q_ref.shape
    hd = q_all.shape[1]
    total = q_all.shape[0]
    x, z, core = place_ref[0], place_ref[1], place_ref[2]
    base, reach = place_ref[3], place_ref[4]
    here = 2 * zs + z
    unit = scale * math.log2(math.e)

    stack_heads(q_all, q_ref)
    stack_heads(do_all, do_ref)
    fill_window(k_win, k_own, k_other, far_own, far_other, z, zs, slice(0, hd), rows)

    near_ok = (x >= 1).astype(F32)
    far_ok = (x >= 2).astype(F32)
    counts = (
        far_own[rows : rows + COUNTS, :hd].astype(F32)
        + far_other[rows : rows + COUNTS, :hd].astype(F32)
    ) * far_ok
    for zz in range(zs):
        both = k_own[zz, 0, rows : rows + COUNTS, :].astype(F32) + k_other[
            zz, 0, rows : rows + COUNTS, :
        ].astype(F32)
        counts = counts + both * near_ok
        both = k_own[zz, 1, rows : rows + COUNTS, :].astype(F32) + k_other[
            zz, 1, rows : rows + COUNTS, :
        ].astype(F32)
        counts = counts + both * jnp.where(zz > z, far_ok, 1.0)
    doc = doc_ref[...]
    first_row = jnp.zeros((1, rows), F32)
    for d in range(1, COUNTS):
        first_row = jnp.where(doc == d, counts[d : d + 1, :rows], first_row)
    first_row = first_row.astype(jnp.int32) + reach
    lo = (jnp.min(first_row) - base) // (2 * rows)
    edge = jnp.minimum((jnp.max(first_row) - base) // (2 * rows) + 1, here)
    info_ref[0] = lo
    pairs = (here - lo + 2) // 2
    start = here + 1 - 2 * pairs
    inner = jnp.minimum((edge - start + 1) // 2, pairs - 1)
    q_pos = base + (here * 2 + core) * rows + lax.broadcasted_iota(jnp.int32, (1, rows), 1)
    firsts = jnp.concatenate([first_row] * (tile // rows), axis=1)
    lasts = jnp.concatenate([q_pos] * (tile // rows), axis=1)
    key_iota = lax.broadcasted_iota(jnp.int32, (rows, tile), 0)

    state[0:1, :] = jnp.full((1, total), NEG_FILL, F32)
    state[1:2, :] = jnp.zeros((1, total), F32)

    def pair_rows(i):
        return pl.ds(pl.multiple_of((start + 2 * i + 1) * 2 * rows, 2 * rows), 4 * rows)

    def visit(i, masked):
        keys = k_win[pair_rows(i), :]
        for t in range(total // tile):
            cols = slice(t * tile, (t + 1) * tile)
            q_t = q_all[cols, :]
            peak = state[0:1, cols]
            for c in range(4):
                cut = slice(c * rows, (c + 1) * rows)
                s = nt(keys[cut], q_t) * unit
                if masked:
                    chip = start + 2 * i + c // 2
                    key_pos = key_iota + (base + (chip * 2 + (core if c % 2 == 0 else 1 - core)) * rows)
                    s = jnp.where((key_pos >= firsts) & (key_pos <= lasts), s, NEG_FILL)
                peak = jnp.maximum(peak, jnp.max(s, axis=0, keepdims=True))
                raw[cut, cols] = s
            factors[i, 0:1, cols] = peak
        for t in range(total // tile):
            cols = slice(t * tile, (t + 1) * tile)
            old, peak = state[0:1, cols], factors[i, 0:1, cols]
            seen = state[1:2, cols] * jnp.exp2(old - peak)
            for c in range(4):
                cut = slice(c * rows, (c + 1) * rows)
                p = jnp.exp2(raw[cut, cols] - peak)
                p_all[i, cut, cols] = p
                seen = seen + jnp.sum(p, axis=0, keepdims=True)
            state[0:1, cols] = peak
            state[1:2, cols] = seen
        pltpu.make_async_copy(p_all.at[i], p_out.at[i], sems.at[i]).start()

    def plain(i, carry):
        visit(i, False)
        return carry

    def edges(i, carry):
        visit(jnp.where(i < inner, i, pairs - 1), True)
        return carry

    lax.fori_loop(0, inner + 1, edges, 0)
    lax.fori_loop(inner, pairs - 1, plain, 0)
    state[1:2, :] = 1.0 / state[1:2, :]

    def second(i, carry):
        dv = None
        for g in range(total // group):
            for t in range(g * group // tile, (g + 1) * group // tile):
                cols = slice(t * tile, (t + 1) * tile)
                factor = jnp.exp2(factors[i, 0:1, cols] - state[0:1, cols]) * state[1:2, cols]
                factors[i, 0:1, cols] = factor
                for c in range(4):
                    cut = slice(c * rows, (c + 1) * rows)
                    low[cut, cols] = (p_all[i, cut, cols] * factor).astype(BF)
            span = slice(g * group, (g + 1) * group)
            more = nn(low[:, span], do_all[span, :])
            dv = more if dv is None else dv + more
        store_pair(start + 2 * i, dv, dv_own, dv_other, z, lambda j: out_index(j, z, zs))
        return carry

    lax.fori_loop(0, pairs, second, 0)

    def clear(j, carry):
        at = out_index(j, z, zs)
        dv_own[at] = jnp.zeros((rows, hd), F32)
        dv_other[at] = jnp.zeros((rows, hd), F32)
        return carry

    lax.fori_loop(z, lo, clear, 0)

    def finish(i, carry):
        pltpu.make_async_copy(p_all.at[i], p_out.at[i], sems.at[i]).wait()
        return carry

    lax.fori_loop(0, pairs, finish, 0)


def score_kernel(
    place_ref,
    info_ref,
    q_ref,
    do_ref,
    o_ref,
    k_own,
    k_other,
    far_own,
    far_other,
    v_own,
    v_other,
    factors,
    owner_ref,
    p_in,
    packed_ref,
    dk_own,
    dk_other,
    q_all,
    do_all,
    k_win,
    v_win,
    p_all,
    low,
    delta,
    dq_sum,
    sems,
    *,
    zs,
    scale,
    tile,
    group,
    block,
):
    rows, width = q_ref.shape
    hd = q_all.shape[1]
    total = q_all.shape[0]
    z = place_ref[1]
    here = 2 * zs + z
    lo = info_ref[0]

    def copy_in(slot):
        return pltpu.make_async_copy(p_in.at[slot], p_all.at[slot], sems.at[slot])

    pairs = (here - lo + 2) // 2
    start = here + 1 - 2 * pairs

    def begin(i, carry):
        copy_in(i).start()
        return carry

    lax.fori_loop(0, pairs, begin, 0)
    stack_heads(q_all, q_ref)
    stack_heads(do_all, do_ref)
    fill_window(k_win, k_own, k_other, far_own, far_other, z, zs, slice(0, hd), rows)
    fill_window(v_win, v_own, v_other, far_own, far_other, z, zs, slice(hd, 2 * hd), rows)
    for n in range(width // hd):
        cols = slice(n * hd, (n + 1) * hd)
        prod = do_ref[:, cols].astype(F32) * o_ref[:, cols].astype(F32)
        delta[0:1, n * rows : (n + 1) * rows] = jnp.sum(prod.T, axis=0, keepdims=True)
    dq_sum[...] = jnp.zeros_like(dq_sum)

    def clear(j, carry):
        at = relative_index(j, z, zs)
        dk_own[at] = jnp.zeros((rows, hd), F32)
        dk_other[at] = jnp.zeros((rows, hd), F32)
        return carry

    lax.fori_loop(z, lo, clear, 0)

    def visit(i, carry):
        copy_in(i).wait()
        window = pl.ds(pl.multiple_of((start + 2 * i + 1) * 2 * rows, 2 * rows), 4 * rows)
        keys_t = k_win[window, :].T
        values = v_win[window, :]
        dk = None
        for g in range(total // group):
            for t in range(g * group // tile, (g + 1) * group // tile):
                cols = slice(t * tile, (t + 1) * tile)
                do_t = do_all[cols, :]
                for c in range(4):
                    cut = slice(c * rows, (c + 1) * rows)
                    dprob = nt(values[cut], do_t)
                    probs = p_all[i, cut, cols] * factors[i, 0:1, cols]
                    low[cut, cols] = (probs * (dprob - delta[0:1, cols]) * scale).astype(BF)
            span = slice(g * group, (g + 1) * group)
            more = nn(low[:, span], q_all[span, :])
            dk = more if dk is None else dk + more
            dq_sum[:, span] += nn(keys_t, low[:, span])
        store_pair(start + 2 * i, dk, dk_own, dk_other, z, lambda j: relative_index(j, z, zs))
        return carry

    lax.fori_loop(0, pairs, visit, 0)
    half_width = width // 2
    half_heads = half_width // hd
    spots = packed_ref.shape[0]
    row = lax.broadcasted_iota(jnp.int32, (spots, rows), 0)
    token = lax.broadcasted_iota(jnp.int32, (spots, rows), 1)
    slots = owner_ref.shape[1]
    spread = lax.broadcasted_iota(jnp.int32, (slots, rows), 1) // block
    spread = spread == lax.broadcasted_iota(jnp.int32, (slots, rows), 0)
    owners = jnp.broadcast_to(owner_ref[...].astype(F32).astype(BF), (8, slots))
    owners = nn(owners, spread.astype(F32).astype(BF))[0:1]
    goes = ((row // (2 * block)).astype(F32) == owners) & (row % block == token % block)
    packed = jnp.zeros((spots, half_width), F32)
    for h in range(2):
        here_half = goes & (row // block % 2 == h)
        turned = [
            dq_sum[:, n * rows : (n + 1) * rows].T.astype(BF)
            for n in range(h * half_heads, (h + 1) * half_heads)
        ]
        packed = packed + nn(here_half.astype(F32).astype(BF), jnp.concatenate(turned, axis=1))
    packed_ref[...] = packed.astype(BF)


def swap(value):
    return lax.ppermute(value, "core", [(0, 1), (1, 0)])


def first_payload_kernel(keys_ref, values_ref, doc_ref, owner_ref, out_ref, notes, *, xs):
    part, groups, hd = keys_ref.shape
    extra, width = notes.shape
    per_device = owner_ref.shape[1]
    row = lax.broadcasted_iota(jnp.int32, (extra, doc_ref.shape[1]), 0)
    earlier = jnp.sum((doc_ref[...] < row).astype(F32), axis=1, keepdims=True)
    notes[...] = jnp.broadcast_to(earlier, (extra, width))
    notes[COUNTS:, :per_device] = jnp.broadcast_to(
        owner_ref[...].astype(F32), (extra - COUNTS, per_device)
    )
    low = notes[...].astype(BF)
    for g in range(groups):
        k, v = keys_ref[:, g, :], values_ref[:, g, :]
        for at in range(g * xs, (g + 1) * xs):
            out_ref[at, :part, :hd] = k
            out_ref[at, :part, hd:] = v
            out_ref[at, part:, :] = low


def pick_kernel(place_ref, k_own, k_other, pick_ref, *, block, per_device, xs):
    zs, _, tall, hd = k_own.shape
    extra = COUNTS + xs
    first = tall - extra
    rows, spots = pick_ref.shape[1:]
    core, me = place_ref[2], place_ref[5]
    slot = lax.broadcasted_iota(jnp.int32, (rows, hd), 0) // block
    to_rows = (slot == lax.broadcasted_iota(jnp.int32, (rows, hd), 1)).astype(F32).astype(BF)
    held = lax.broadcasted_iota(jnp.int32, (zs * extra, hd), 0) % extra >= COUNTS
    held = held & (lax.broadcasted_iota(jnp.int32, (zs * extra, hd), 1) < per_device)
    line = lax.broadcasted_iota(jnp.int32, (zs * extra, spots), 0)
    peer = lax.broadcasted_iota(jnp.int32, (zs * extra, spots), 1) // (2 * block)
    pick = jnp.zeros((rows, spots), F32)
    for notes, c in ((k_own, core), (k_other, 1 - core)):
        owners = jnp.concatenate([notes[zz, 0, first:, :].astype(F32) for zz in range(zs)], axis=0)
        hit = (held & (owners == me.astype(F32))).astype(F32).astype(BF)
        source = ((line % extra - COUNTS) * zs + line // extra) * 2 + c
        to_spots = ((source == peer) & (line % extra >= COUNTS)).astype(F32).astype(BF)
        pick = pick + nn(nt(to_rows, hit).astype(BF), to_spots)
    row = lax.broadcasted_iota(jnp.int32, (rows, spots), 0)
    spot = lax.broadcasted_iota(jnp.int32, (rows, spots), 1)
    same = spot % block == row % block
    for h in range(2):
        pick_ref[h] = jnp.where(same & (spot // block % 2 == h), pick, 0.0).astype(BF)


def placement_kernel(pick_ref, arrived_ref, out_ref):
    half_width = arrived_ref.shape[1]
    for h in range(2):
        out_ref[:, h * half_width : (h + 1) * half_width] = nn(
            pick_ref[h], arrived_ref[...]
        ).astype(BF)


def along_x(parts, xs):
    mine, near, far = parts
    from_next = lax.ppermute(near, "x", [(i, i - 1) for i in range(1, xs)])
    from_last = lax.ppermute(far, "x", [(i, i - 2) for i in range(2, xs)])
    return (mine + from_next + from_last).astype(BF)


def reduce_at_once(own, other, zs):
    rows, hd = own.shape[1:]
    swapped = swap(other)
    sent = (own[: 2 * zs] + swapped[: 2 * zs]).astype(BF).reshape(zs, 2, rows, hd)
    came = lax.all_to_all(sent, "z", split_axis=0, concat_axis=0, tiled=True)
    return came, own[2 * zs] + swapped[2 * zs]


def sum_arrived(came, far, zs, z):
    came = came.astype(F32)
    later = (jnp.arange(zs) >= z)[:, None, None]
    mine = jnp.sum(jnp.where(later, came[:, 1], 0.0), axis=0)
    near = jnp.sum(came[:, 0], axis=0)
    far = jnp.sum(jnp.where(later, 0.0, came[:, 1]), axis=0) + far
    return mine, near, far


def reduce_by_shifts(own, other, zs, z):
    swapped = swap(other)
    came = []
    for k in range(1, zs):
        sent = (own[2 * k : 2 * k + 2] + swapped[2 * k : 2 * k + 2]).astype(BF)
        came.append(lax.ppermute(sent, "z", [(i, (i + k) % zs) for i in range(zs)]))
    mine = own[1] + swapped[1]
    near = own[0] + swapped[0]
    far = own[2 * zs] + swapped[2 * zs]
    for k, got in enumerate(came, 1):
        near = near + got[0].astype(F32)
        mine = mine + jnp.where(z < k, got[1].astype(F32), 0.0)
        far = far + jnp.where(z < k, 0.0, got[1].astype(F32))
    return mine, near, far, came[zs // 2]


def program(queries, keys, values, outputs, grad_out, doc_ids, owner):
    hd = keys.shape[2]
    scale = hd**-0.5
    rows, _, width = queries.shape
    total = rows * (width // hd)
    tile = min(256, total)
    group = min(1024, total)
    xs, zs = lax.axis_size("x"), lax.axis_size("z")
    x, z, core = lax.axis_index("x"), lax.axis_index("z"), lax.axis_index("core")
    peers = xs * zs * 2
    per_device = owner.shape[0]
    block_len = rows // per_device
    part = keys.shape[0]
    chips = 2 * zs + 1
    steps = zs + 1

    extra = COUNTS + xs
    vmem = pl.BlockSpec(memory_space=pltpu.VMEM)
    smem = pl.BlockSpec(memory_space=pltpu.SMEM)
    anywhere = pl.BlockSpec(memory_space=pl.ANY)
    mixed = pl.pallas_call(
        functools.partial(first_payload_kernel, xs=xs),
        in_specs=[vmem] * 4,
        out_specs=vmem,
        out_shape=jax.ShapeDtypeStruct((4 * xs, part + extra, 2 * hd), BF),
        scratch_shapes=[pltpu.VMEM((extra, 2 * hd), F32)],
        name="first_payload",
    )(keys, values, doc_ids[None], owner[None])
    mixed = lax.all_to_all(
        mixed,
        ("dp", "head", "x"),
        split_axis=0,
        concat_axis=0,
        tiled=True,
    ).reshape(2, 2, xs, part + extra, 2 * hd)

    def piece(back):
        got = lax.dynamic_index_in_dim(mixed, lax.rem(x - back + xs, xs), 2, keepdims=False)
        tokens = jnp.transpose(got[:, :, :part], (1, 0, 2, 3)).reshape(rows, 2 * hd)
        return jnp.concatenate([tokens, got[0, 0, part:]], axis=0)

    last, near, far = piece(0), piece(1), piece(2)
    far_other = swap(far)

    def along_z(a, b, c):
        ahead = (jnp.arange(zs) >= z)[:, None, None]
        chosen = jnp.where(ahead, a[None], c[None])
        pair = jnp.stack([jnp.broadcast_to(b[None], chosen.shape), chosen], axis=1)
        return lax.all_to_all(pair, "z", split_axis=0, concat_axis=0, tiled=True)

    held = mixed[0, 0, :, part + COUNTS, :hd]
    near_keys = jnp.concatenate([near[: rows + COUNTS, :hd], held], axis=0)
    k_own = along_z(last[:, :hd], near_keys, far[:, :hd])
    k_other = swap(k_own)
    v_own = along_z(last[:rows, hd:], near[:rows, hd:], far[:rows, hd:])

    base = (x - 2) * (zs * 2 * rows)
    me = (x * zs + z) * 2 + core
    place = jnp.stack([x, z, core, base, jnp.maximum(base + z * 2 * rows, 0), me]).astype(jnp.int32)
    q = queries.reshape(rows, width)
    do = grad_out.reshape(rows, width)
    o = outputs.reshape(rows, width)
    grad_shape = jax.ShapeDtypeStruct((chips, rows, hd), F32)
    params = pltpu.CompilerParams(vmem_limit_bytes=VMEM_BYTES)
    small = pltpu.CompilerParams(vmem_limit_bytes=8 * 1024 * 1024)
    dv_own, dv_other, probs, info, factors = pl.pallas_call(
        functools.partial(softmax_kernel, zs=zs, scale=scale, tile=tile, group=group),
        in_specs=[smem] + [vmem] * 7,
        out_specs=[vmem, vmem, anywhere, smem, vmem],
        out_shape=[
            grad_shape,
            grad_shape,
            jax.ShapeDtypeStruct((steps, 4 * rows, total), F32),
            jax.ShapeDtypeStruct((1,), jnp.int32),
            jax.ShapeDtypeStruct((steps, 8, total), F32),
        ],
        scratch_shapes=[
            pltpu.VMEM((total, hd), BF),
            pltpu.VMEM((total, hd), BF),
            pltpu.VMEM(((3 * zs + 1) * 2 * rows, hd), BF),
            pltpu.VMEM((steps, 4 * rows, total), F32),
            pltpu.VMEM((4 * rows, total), F32),
            pltpu.VMEM((4 * rows, total), BF),
            pltpu.VMEM((8, total), F32),
            pltpu.SemaphoreType.DMA((steps,)),
        ],
        compiler_params=params,
        cost_estimate=pl.CostEstimate(
            flops=12_000_000_000, bytes_accessed=20_000_000, transcendentals=4_000_000
        ),
        name="softmax_and_value_gradient",
    )(
        place,
        q,
        do,
        doc_ids.reshape(1, rows),
        k_own,
        k_other,
        far,
        far_other,
    )
    v_other = swap(v_own)
    came_v, far_v = reduce_at_once(dv_own, dv_other, zs)
    packed, dk_own, dk_other = pl.pallas_call(
        functools.partial(
            score_kernel, zs=zs, scale=scale, tile=tile, group=group, block=block_len
        ),
        in_specs=[smem, smem] + [vmem] * 11 + [anywhere],
        out_specs=[vmem] * 3,
        out_shape=[
            jax.ShapeDtypeStruct((peers * 2 * block_len, width // 2), BF),
            grad_shape,
            grad_shape,
        ],
        scratch_shapes=[
            pltpu.VMEM((total, hd), BF),
            pltpu.VMEM((total, hd), BF),
            pltpu.VMEM(((3 * zs + 1) * 2 * rows, hd), BF),
            pltpu.VMEM(((3 * zs + 1) * 2 * rows, hd), BF),
            pltpu.VMEM((steps, 4 * rows, total), F32),
            pltpu.VMEM((4 * rows, total), BF),
            pltpu.VMEM((8, total), F32),
            pltpu.VMEM((hd, total), F32),
            pltpu.SemaphoreType.DMA((steps,)),
        ],
        compiler_params=params,
        cost_estimate=pl.CostEstimate(
            flops=12_000_000_000, bytes_accessed=20_000_000, transcendentals=0
        ),
        name="score_gradient",
    )(
        place,
        info,
        q,
        do,
        o,
        k_own,
        k_other,
        far,
        far_other,
        v_own,
        v_other,
        factors,
        owner[None],
        probs,
    )
    *parts_k, halfway = reduce_by_shifts(dk_own, dk_other, zs, z)
    parts_v = sum_arrived(lax.optimization_barrier((came_v, halfway))[0], far_v, zs, z)
    grads = along_x([jnp.concatenate(pair, axis=1) for pair in zip(parts_k, parts_v)], xs)
    grad_k, grad_v = grads[:, None, :hd], grads[:, None, hd:]

    pick = pl.pallas_call(
        functools.partial(pick_kernel, block=block_len, per_device=per_device, xs=xs),
        in_specs=[smem, vmem, vmem],
        out_specs=vmem,
        out_shape=jax.ShapeDtypeStruct((2, rows, peers * 2 * block_len), BF),
        cost_estimate=pl.CostEstimate(flops=100_000_000, bytes_accessed=1_000_000, transcendentals=0),
        compiler_params=small,
        name="placement_choice",
    )(lax.optimization_barrier((place, halfway))[0], k_own, k_other)
    arrived = lax.all_to_all(
        packed.reshape(peers, 2 * block_len, width // 2),
        ("x", "z", "core"),
        split_axis=0,
        concat_axis=0,
        tiled=True,
    )
    placed = pl.pallas_call(
        placement_kernel,
        in_specs=[vmem, vmem],
        out_specs=vmem,
        out_shape=jax.ShapeDtypeStruct((rows, width), BF),
        compiler_params=small,
        name="query_gradient_placement",
    )(pick, arrived.reshape(packed.shape))
    return (placed.reshape(rows, 1, width), grad_k, grad_v)


def solution(mesh):
    sizes = mesh.shape
    dp, ctx, head = sizes["dp"], sizes["ctx"], sizes["head"]
    xs = 4
    fine = Mesh(
        mesh.devices.reshape(dp, xs, ctx // (2 * xs), 2, head), ("dp", "x", "z", "core", "head")
    )
    ctx_axes = ("x", "z", "core")
    heads = P(ctx_axes, ("dp", "head"), None)
    tokens = P(ctx_axes + ("head", "dp"), None, None)
    return jax.shard_map(
        program,
        mesh=fine,
        in_specs=(heads, tokens, tokens, heads, heads, P(ctx_axes), P(ctx_axes)),
        out_specs=(heads, heads, heads),
        check_vma=False,
    )
```

```python
import functools
import math

import jax
import jax.numpy as jnp
from jax import lax
from jax.experimental import pallas as pl
from jax.experimental.pallas import tpu as pltpu
from jax.sharding import Mesh, PartitionSpec as P


NEG_FILL = -1e30
VMEM_BYTES = 60 * 1024 * 1024
BF = jnp.bfloat16
F32 = jnp.float32
COUNTS = 4


def nt(a, b):
    return lax.dot_general(a, b, (((1,), (1,)), ((), ())), preferred_element_type=F32)


def nn(a, b):
    return lax.dot_general(a, b, (((1,), (0,)), ((), ())), preferred_element_type=F32)


def stack_heads(dst, src):
    rows, width = src.shape
    hd = dst.shape[1]
    for n in range(width // hd):
        dst[n * rows : (n + 1) * rows, :] = src[:, n * hd : (n + 1) * hd]


def fill_window(win, own, other, far_own, far_other, z, zs, cols, rows):
    hd = win.shape[1]

    def at(j, half):
        start = (j + 1) * 2 * rows + half * rows
        return pl.ds(start if isinstance(start, int) else pl.multiple_of(start, rows), rows)

    for half, near, far in ((0, own, far_own), (1, other, far_other)):
        for zz in range(zs):
            win[at(zs + zz, half), :] = near[zz, 0, :rows, :]
            win[at(jnp.where(zz > z, zz, 2 * zs + zz), half), :] = near[zz, 1, :rows, :]
        win[at(z, half), :] = far[:rows, cols]
        win[at(z - 1, half), :] = jnp.zeros((rows, hd), BF)


def out_index(j, z, zs):
    zz = lax.rem(j, zs)
    middle = (j >= zs) & (j < 2 * zs)
    return jnp.where(middle, 2 * zz, jnp.where(j == z, 2 * zs, 2 * zz + 1))


def relative_index(j, z, zs):
    zz = lax.rem(lax.rem(j, zs) + zs - z, zs)
    middle = (j >= zs) & (j < 2 * zs)
    return jnp.where(middle, 2 * zz, jnp.where(j == z, 2 * zs, 2 * zz + 1))


def store_pair(j, value, own, other, z, index):
    rows = own.shape[1]

    @pl.when(j >= z)
    def _():
        own[index(j)] = value[:rows]
        other[index(j)] = value[rows : 2 * rows].astype(other.dtype)

    own[index(j + 1)] = value[2 * rows : 3 * rows]
    other[index(j + 1)] = value[3 * rows :].astype(other.dtype)


def softmax_kernel(
    place_ref,
    q_ref,
    do_ref,
    doc_ref,
    k_own,
    k_other,
    far_own,
    far_other,
    dv_own,
    dv_other,
    p_out,
    info_ref,
    factors,
    q_all,
    do_all,
    k_win,
    p_all,
    raw,
    low,
    state,
    sems,
    *,
    zs,
    scale,
    tile,
    group,
):
    rows, _ = q_ref.shape
    hd = q_all.shape[1]
    total = q_all.shape[0]
    x, z, core = place_ref[0], place_ref[1], place_ref[2]
    base, reach = place_ref[3], place_ref[4]
    here = 2 * zs + z
    unit = scale * math.log2(math.e)

    stack_heads(q_all, q_ref)
    stack_heads(do_all, do_ref)
    fill_window(k_win, k_own, k_other, far_own, far_other, z, zs, slice(0, hd), rows)

    near_ok = (x >= 1).astype(F32)
    far_ok = (x >= 2).astype(F32)
    counts = (
        far_own[rows : rows + COUNTS, :hd].astype(F32)
        + far_other[rows : rows + COUNTS, :hd].astype(F32)
    ) * far_ok
    for zz in range(zs):
        both = k_own[zz, 0, rows : rows + COUNTS, :].astype(F32) + k_other[
            zz, 0, rows : rows + COUNTS, :
        ].astype(F32)
        counts = counts + both * near_ok
        both = k_own[zz, 1, rows : rows + COUNTS, :].astype(F32) + k_other[
            zz, 1, rows : rows + COUNTS, :
        ].astype(F32)
        counts = counts + both * jnp.where(zz > z, far_ok, 1.0)
    doc = doc_ref[...]
    first_row = jnp.zeros((1, rows), F32)
    for d in range(1, COUNTS):
        first_row = jnp.where(doc == d, counts[d : d + 1, :rows], first_row)
    first_row = first_row.astype(jnp.int32) + reach
    lo = (jnp.min(first_row) - base) // (2 * rows)
    edge = jnp.minimum((jnp.max(first_row) - base) // (2 * rows) + 1, here)
    info_ref[0] = lo
    pairs = (here - lo + 2) // 2
    start = here + 1 - 2 * pairs
    inner = jnp.minimum((edge - start + 1) // 2, pairs - 1)
    q_pos = base + (here * 2 + core) * rows + lax.broadcasted_iota(jnp.int32, (1, rows), 1)
    firsts = jnp.concatenate([first_row] * (tile // rows), axis=1)
    lasts = jnp.concatenate([q_pos] * (tile // rows), axis=1)
    key_iota = lax.broadcasted_iota(jnp.int32, (rows, tile), 0)

    state[0:1, :] = jnp.full((1, total), NEG_FILL, F32)
    state[1:2, :] = jnp.zeros((1, total), F32)

    def pair_rows(i):
        return pl.ds(pl.multiple_of((start + 2 * i + 1) * 2 * rows, 2 * rows), 4 * rows)

    def visit(i, masked):
        keys = k_win[pair_rows(i), :]
        for t in range(total // tile):
            cols = slice(t * tile, (t + 1) * tile)
            q_t = q_all[cols, :]
            peak = state[0:1, cols]
            for c in range(4):
                cut = slice(c * rows, (c + 1) * rows)
                s = nt(keys[cut], q_t) * unit
                if masked:
                    chip = start + 2 * i + c // 2
                    key_pos = key_iota + (base + (chip * 2 + (core if c % 2 == 0 else 1 - core)) * rows)
                    s = jnp.where((key_pos >= firsts) & (key_pos <= lasts), s, NEG_FILL)
                peak = jnp.maximum(peak, jnp.max(s, axis=0, keepdims=True))
                raw[cut, cols] = s
            factors[i, 0:1, cols] = peak
        for t in range(total // tile):
            cols = slice(t * tile, (t + 1) * tile)
            old, peak = state[0:1, cols], factors[i, 0:1, cols]
            seen = state[1:2, cols] * jnp.exp2(old - peak)
            for c in range(4):
                cut = slice(c * rows, (c + 1) * rows)
                p = jnp.exp2(raw[cut, cols] - peak)
                p_all[i, cut, cols] = p
                seen = seen + jnp.sum(p, axis=0, keepdims=True)
            state[0:1, cols] = peak
            state[1:2, cols] = seen
        pltpu.make_async_copy(p_all.at[i], p_out.at[i], sems.at[i]).start()

    def plain(i, carry):
        visit(i, False)
        return carry

    def edges(i, carry):
        visit(jnp.where(i < inner, i, pairs - 1), True)
        return carry

    lax.fori_loop(0, inner + 1, edges, 0)
    lax.fori_loop(inner, pairs - 1, plain, 0)
    state[1:2, :] = 1.0 / state[1:2, :]

    def second(i, carry):
        dv = None
        for g in range(total // group):
            for t in range(g * group // tile, (g + 1) * group // tile):
                cols = slice(t * tile, (t + 1) * tile)
                factor = jnp.exp2(factors[i, 0:1, cols] - state[0:1, cols]) * state[1:2, cols]
                factors[i, 0:1, cols] = factor
                for c in range(4):
                    cut = slice(c * rows, (c + 1) * rows)
                    low[cut, cols] = (p_all[i, cut, cols] * factor).astype(BF)
            span = slice(g * group, (g + 1) * group)
            more = nn(low[:, span], do_all[span, :])
            dv = more if dv is None else dv + more
        store_pair(start + 2 * i, dv, dv_own, dv_other, z, lambda j: out_index(j, z, zs))
        return carry

    lax.fori_loop(0, pairs, second, 0)

    def clear(j, carry):
        at = out_index(j, z, zs)
        dv_own[at] = jnp.zeros((rows, hd), F32)
        dv_other[at] = jnp.zeros((rows, hd), BF)
        return carry

    lax.fori_loop(z, lo, clear, 0)

    def finish(i, carry):
        pltpu.make_async_copy(p_all.at[i], p_out.at[i], sems.at[i]).wait()
        return carry

    lax.fori_loop(0, pairs, finish, 0)


def score_kernel(
    place_ref,
    info_ref,
    q_ref,
    do_ref,
    o_ref,
    k_own,
    k_other,
    far_own,
    far_other,
    v_own,
    v_other,
    factors,
    owner_ref,
    p_in,
    packed_ref,
    dk_own,
    dk_other,
    q_all,
    do_all,
    k_win,
    v_win,
    p_all,
    low,
    delta,
    dq_sum,
    sems,
    *,
    zs,
    scale,
    tile,
    group,
    block,
):
    rows, width = q_ref.shape
    hd = q_all.shape[1]
    total = q_all.shape[0]
    z = place_ref[1]
    here = 2 * zs + z
    lo = info_ref[0]

    def copy_in(slot):
        return pltpu.make_async_copy(p_in.at[slot], p_all.at[slot], sems.at[slot])

    pairs = (here - lo + 2) // 2
    start = here + 1 - 2 * pairs

    def begin(i, carry):
        copy_in(i).start()
        return carry

    lax.fori_loop(0, pairs, begin, 0)
    stack_heads(q_all, q_ref)
    stack_heads(do_all, do_ref)
    fill_window(k_win, k_own, k_other, far_own, far_other, z, zs, slice(0, hd), rows)
    fill_window(v_win, v_own, v_other, far_own, far_other, z, zs, slice(hd, 2 * hd), rows)
    for n in range(width // hd):
        cols = slice(n * hd, (n + 1) * hd)
        prod = do_ref[:, cols].astype(F32) * o_ref[:, cols].astype(F32)
        delta[0:1, n * rows : (n + 1) * rows] = jnp.sum(prod.T, axis=0, keepdims=True)
    dq_sum[...] = jnp.zeros_like(dq_sum)

    def clear(j, carry):
        at = relative_index(j, z, zs)
        dk_own[at] = jnp.zeros((rows, hd), F32)
        dk_other[at] = jnp.zeros((rows, hd), BF)
        return carry

    lax.fori_loop(z, lo, clear, 0)

    def visit(i, carry):
        copy_in(i).wait()
        window = pl.ds(pl.multiple_of((start + 2 * i + 1) * 2 * rows, 2 * rows), 4 * rows)
        keys_t = k_win[window, :].T
        values = v_win[window, :]
        dk = None
        for g in range(total // group):
            for t in range(g * group // tile, (g + 1) * group // tile):
                cols = slice(t * tile, (t + 1) * tile)
                do_t = do_all[cols, :]
                for c in range(4):
                    cut = slice(c * rows, (c + 1) * rows)
                    dprob = nt(values[cut], do_t)
                    probs = p_all[i, cut, cols] * factors[i, 0:1, cols]
                    low[cut, cols] = (probs * (dprob - delta[0:1, cols]) * scale).astype(BF)
            span = slice(g * group, (g + 1) * group)
            more = nn(low[:, span], q_all[span, :])
            dk = more if dk is None else dk + more
            dq_sum[:, span] += nn(keys_t, low[:, span])
        store_pair(start + 2 * i, dk, dk_own, dk_other, z, lambda j: relative_index(j, z, zs))
        return carry

    lax.fori_loop(0, pairs, visit, 0)
    half_width = width // 2
    half_heads = half_width // hd
    spots = packed_ref.shape[0]
    row = lax.broadcasted_iota(jnp.int32, (spots, rows), 0)
    token = lax.broadcasted_iota(jnp.int32, (spots, rows), 1)
    slots = owner_ref.shape[1]
    spread = lax.broadcasted_iota(jnp.int32, (slots, rows), 1) // block
    spread = spread == lax.broadcasted_iota(jnp.int32, (slots, rows), 0)
    owners = jnp.broadcast_to(owner_ref[...].astype(F32).astype(BF), (8, slots))
    owners = nn(owners, spread.astype(F32).astype(BF))[0:1]
    goes = ((row // (2 * block)).astype(F32) == owners) & (row % block == token % block)
    packed = jnp.zeros((spots, half_width), F32)
    for h in range(2):
        here_half = goes & (row // block % 2 == h)
        turned = [
            dq_sum[:, n * rows : (n + 1) * rows].T.astype(BF)
            for n in range(h * half_heads, (h + 1) * half_heads)
        ]
        packed = packed + nn(here_half.astype(F32).astype(BF), jnp.concatenate(turned, axis=1))
    packed_ref[...] = packed.astype(BF)


def swap(value):
    return lax.ppermute(value, "core", [(0, 1), (1, 0)])


def first_payload_kernel(keys_ref, values_ref, doc_ref, owner_ref, out_ref, notes, *, xs):
    part, groups, hd = keys_ref.shape
    extra, width = notes.shape
    per_device = owner_ref.shape[1]
    row = lax.broadcasted_iota(jnp.int32, (extra, doc_ref.shape[1]), 0)
    earlier = jnp.sum((doc_ref[...] < row).astype(F32), axis=1, keepdims=True)
    notes[...] = jnp.broadcast_to(earlier, (extra, width))
    notes[COUNTS:, :per_device] = jnp.broadcast_to(
        owner_ref[...].astype(F32), (extra - COUNTS, per_device)
    )
    low = notes[...].astype(BF)
    for g in range(groups):
        k, v = keys_ref[:, g, :], values_ref[:, g, :]
        for at in range(g * xs, (g + 1) * xs):
            out_ref[at, :part, :hd] = k
            out_ref[at, :part, hd:] = v
            out_ref[at, part:, :] = low


def pick_kernel(place_ref, k_own, k_other, pick_ref, *, block, per_device, xs):
    zs, _, tall, hd = k_own.shape
    extra = COUNTS + xs
    first = tall - extra
    rows, spots = pick_ref.shape[1:]
    core, me = place_ref[2], place_ref[5]
    slot = lax.broadcasted_iota(jnp.int32, (rows, hd), 0) // block
    to_rows = (slot == lax.broadcasted_iota(jnp.int32, (rows, hd), 1)).astype(F32).astype(BF)
    held = lax.broadcasted_iota(jnp.int32, (zs * extra, hd), 0) % extra >= COUNTS
    held = held & (lax.broadcasted_iota(jnp.int32, (zs * extra, hd), 1) < per_device)
    line = lax.broadcasted_iota(jnp.int32, (zs * extra, spots), 0)
    peer = lax.broadcasted_iota(jnp.int32, (zs * extra, spots), 1) // (2 * block)
    pick = jnp.zeros((rows, spots), F32)
    for notes, c in ((k_own, core), (k_other, 1 - core)):
        owners = jnp.concatenate([notes[zz, 0, first:, :].astype(F32) for zz in range(zs)], axis=0)
        hit = (held & (owners == me.astype(F32))).astype(F32).astype(BF)
        source = ((line % extra - COUNTS) * zs + line // extra) * 2 + c
        to_spots = ((source == peer) & (line % extra >= COUNTS)).astype(F32).astype(BF)
        pick = pick + nn(nt(to_rows, hit).astype(BF), to_spots)
    row = lax.broadcasted_iota(jnp.int32, (rows, spots), 0)
    spot = lax.broadcasted_iota(jnp.int32, (rows, spots), 1)
    same = spot % block == row % block
    for h in range(2):
        pick_ref[h] = jnp.where(same & (spot // block % 2 == h), pick, 0.0).astype(BF)


def placement_kernel(pick_ref, arrived_ref, out_ref):
    half_width = arrived_ref.shape[1]
    for h in range(2):
        out_ref[:, h * half_width : (h + 1) * half_width] = nn(
            pick_ref[h], arrived_ref[...]
        ).astype(BF)


def along_x(parts, xs):
    mine, near, far = parts
    from_next = lax.ppermute(near, "x", [(i, i - 1) for i in range(1, xs)])
    from_last = lax.ppermute(far, "x", [(i, i - 2) for i in range(2, xs)])
    return (mine + from_next + from_last).astype(BF)


def reduce_at_once(own, other, zs):
    rows, hd = own.shape[1:]
    swapped = swap(other)
    sent = (own[: 2 * zs] + swapped[: 2 * zs].astype(F32)).astype(BF).reshape(zs, 2, rows, hd)
    came = lax.all_to_all(sent, "z", split_axis=0, concat_axis=0, tiled=True)
    return came, own[2 * zs] + swapped[2 * zs].astype(F32)


def sum_arrived(came, far, zs, z):
    came = came.astype(F32)
    later = (jnp.arange(zs) >= z)[:, None, None]
    mine = jnp.sum(jnp.where(later, came[:, 1], 0.0), axis=0)
    near = jnp.sum(came[:, 0], axis=0)
    far = jnp.sum(jnp.where(later, 0.0, came[:, 1]), axis=0) + far
    return mine, near, far


def reduce_by_shifts(own, other, zs, z):
    swapped = swap(other)

    def both(at):
        return own[at] + swapped[at].astype(F32)

    came = []
    for k in range(1, zs):
        sent = both(slice(2 * k, 2 * k + 2)).astype(BF)
        came.append(lax.ppermute(sent, "z", [(i, (i + k) % zs) for i in range(zs)]))
    mine, near, far = both(1), both(0), both(2 * zs)
    for k, got in enumerate(came, 1):
        near = near + got[0].astype(F32)
        mine = mine + jnp.where(z < k, got[1].astype(F32), 0.0)
        far = far + jnp.where(z < k, 0.0, got[1].astype(F32))
    return mine, near, far, came[zs // 2]


def program(queries, keys, values, outputs, grad_out, doc_ids, owner):
    hd = keys.shape[2]
    scale = hd**-0.5
    rows, _, width = queries.shape
    total = rows * (width // hd)
    tile = min(256, total)
    group = min(1024, total)
    xs, zs = lax.axis_size("x"), lax.axis_size("z")
    x, z, core = lax.axis_index("x"), lax.axis_index("z"), lax.axis_index("core")
    peers = xs * zs * 2
    per_device = owner.shape[0]
    block_len = rows // per_device
    part = keys.shape[0]
    chips = 2 * zs + 1
    steps = zs + 1

    extra = COUNTS + xs
    vmem = pl.BlockSpec(memory_space=pltpu.VMEM)
    smem = pl.BlockSpec(memory_space=pltpu.SMEM)
    anywhere = pl.BlockSpec(memory_space=pl.ANY)
    mixed = pl.pallas_call(
        functools.partial(first_payload_kernel, xs=xs),
        in_specs=[vmem] * 4,
        out_specs=vmem,
        out_shape=jax.ShapeDtypeStruct((4 * xs, part + extra, 2 * hd), BF),
        scratch_shapes=[pltpu.VMEM((extra, 2 * hd), F32)],
        name="first_payload",
    )(keys, values, doc_ids[None], owner[None])
    mixed = lax.all_to_all(
        mixed,
        ("dp", "head", "x"),
        split_axis=0,
        concat_axis=0,
        tiled=True,
    ).reshape(2, 2, xs, part + extra, 2 * hd)

    def piece(back):
        got = lax.dynamic_index_in_dim(mixed, lax.rem(x - back + xs, xs), 2, keepdims=False)
        tokens = jnp.transpose(got[:, :, :part], (1, 0, 2, 3)).reshape(rows, 2 * hd)
        return jnp.concatenate([tokens, got[0, 0, part:]], axis=0)

    last, near, far = piece(0), piece(1), piece(2)
    far_other = swap(far)

    def along_z(a, b, c):
        ahead = (jnp.arange(zs) >= z)[:, None, None]
        chosen = jnp.where(ahead, a[None], c[None])
        pair = jnp.stack([jnp.broadcast_to(b[None], chosen.shape), chosen], axis=1)
        return lax.all_to_all(pair, "z", split_axis=0, concat_axis=0, tiled=True)

    held = mixed[0, 0, :, part + COUNTS, :hd]
    near_keys = jnp.concatenate([near[: rows + COUNTS, :hd], held], axis=0)
    k_own = along_z(last[:, :hd], near_keys, far[:, :hd])
    k_other = swap(k_own)
    v_own = along_z(last[:rows, hd:], near[:rows, hd:], far[:rows, hd:])

    base = (x - 2) * (zs * 2 * rows)
    me = (x * zs + z) * 2 + core
    place = jnp.stack([x, z, core, base, jnp.maximum(base + z * 2 * rows, 0), me]).astype(jnp.int32)
    q = queries.reshape(rows, width)
    do = grad_out.reshape(rows, width)
    o = outputs.reshape(rows, width)
    own_shape = jax.ShapeDtypeStruct((chips, rows, hd), F32)
    other_shape = jax.ShapeDtypeStruct((chips, rows, hd), BF)
    params = pltpu.CompilerParams(vmem_limit_bytes=VMEM_BYTES)
    small = pltpu.CompilerParams(vmem_limit_bytes=8 * 1024 * 1024)
    dv_own, dv_other, probs, info, factors = pl.pallas_call(
        functools.partial(softmax_kernel, zs=zs, scale=scale, tile=tile, group=group),
        in_specs=[smem] + [vmem] * 7,
        out_specs=[vmem, vmem, anywhere, smem, vmem],
        out_shape=[
            own_shape,
            other_shape,
            jax.ShapeDtypeStruct((steps, 4 * rows, total), F32),
            jax.ShapeDtypeStruct((1,), jnp.int32),
            jax.ShapeDtypeStruct((steps, 8, total), F32),
        ],
        scratch_shapes=[
            pltpu.VMEM((total, hd), BF),
            pltpu.VMEM((total, hd), BF),
            pltpu.VMEM(((3 * zs + 1) * 2 * rows, hd), BF),
            pltpu.VMEM((steps, 4 * rows, total), F32),
            pltpu.VMEM((4 * rows, total), F32),
            pltpu.VMEM((4 * rows, total), BF),
            pltpu.VMEM((8, total), F32),
            pltpu.SemaphoreType.DMA((steps,)),
        ],
        compiler_params=params,
        cost_estimate=pl.CostEstimate(
            flops=12_000_000_000, bytes_accessed=20_000_000, transcendentals=4_000_000
        ),
        name="softmax_and_value_gradient",
    )(
        place,
        q,
        do,
        doc_ids.reshape(1, rows),
        k_own,
        k_other,
        far,
        far_other,
    )
    v_other = swap(v_own)
    came_v, far_v = reduce_at_once(dv_own, dv_other, zs)
    packed, dk_own, dk_other = pl.pallas_call(
        functools.partial(
            score_kernel, zs=zs, scale=scale, tile=tile, group=group, block=block_len
        ),
        in_specs=[smem, smem] + [vmem] * 11 + [anywhere],
        out_specs=[vmem] * 3,
        out_shape=[
            jax.ShapeDtypeStruct((peers * 2 * block_len, width // 2), BF),
            own_shape,
            other_shape,
        ],
        scratch_shapes=[
            pltpu.VMEM((total, hd), BF),
            pltpu.VMEM((total, hd), BF),
            pltpu.VMEM(((3 * zs + 1) * 2 * rows, hd), BF),
            pltpu.VMEM(((3 * zs + 1) * 2 * rows, hd), BF),
            pltpu.VMEM((steps, 4 * rows, total), F32),
            pltpu.VMEM((4 * rows, total), BF),
            pltpu.VMEM((8, total), F32),
            pltpu.VMEM((hd, total), F32),
            pltpu.SemaphoreType.DMA((steps,)),
        ],
        compiler_params=params,
        cost_estimate=pl.CostEstimate(
            flops=12_000_000_000, bytes_accessed=20_000_000, transcendentals=0
        ),
        name="score_gradient",
    )(
        place,
        info,
        q,
        do,
        o,
        k_own,
        k_other,
        far,
        far_other,
        v_own,
        v_other,
        factors,
        owner[None],
        probs,
    )
    *parts_k, halfway = reduce_by_shifts(dk_own, dk_other, zs, z)
    parts_v = sum_arrived(lax.optimization_barrier((came_v, halfway))[0], far_v, zs, z)
    grads = along_x([jnp.concatenate(pair, axis=1) for pair in zip(parts_k, parts_v)], xs)
    grad_k, grad_v = grads[:, None, :hd], grads[:, None, hd:]

    pick = pl.pallas_call(
        functools.partial(pick_kernel, block=block_len, per_device=per_device, xs=xs),
        in_specs=[smem, vmem, vmem],
        out_specs=vmem,
        out_shape=jax.ShapeDtypeStruct((2, rows, peers * 2 * block_len), BF),
        cost_estimate=pl.CostEstimate(flops=100_000_000, bytes_accessed=1_000_000, transcendentals=0),
        compiler_params=small,
        name="placement_choice",
    )(place, k_own, k_other)
    arrived = lax.all_to_all(
        packed.reshape(peers, 2 * block_len, width // 2),
        ("x", "z", "core"),
        split_axis=0,
        concat_axis=0,
        tiled=True,
    )
    placed = pl.pallas_call(
        placement_kernel,
        in_specs=[vmem, vmem],
        out_specs=vmem,
        out_shape=jax.ShapeDtypeStruct((rows, width), BF),
        compiler_params=small,
        name="query_gradient_placement",
    )(pick, arrived.reshape(packed.shape))
    return (placed.reshape(rows, 1, width), grad_k, grad_v)


def solution(mesh):
    sizes = mesh.shape
    dp, ctx, head = sizes["dp"], sizes["ctx"], sizes["head"]
    xs = 4
    fine = Mesh(
        mesh.devices.reshape(dp, xs, ctx // (2 * xs), 2, head), ("dp", "x", "z", "core", "head")
    )
    ctx_axes = ("x", "z", "core")
    heads = P(ctx_axes, ("dp", "head"), None)
    tokens = P(ctx_axes + ("head", "dp"), None, None)
    return jax.shard_map(
        program,
        mesh=fine,
        in_specs=(heads, tokens, tokens, heads, heads, P(ctx_axes), P(ctx_axes)),
        out_specs=(heads, heads, heads),
        check_vma=False,
    )
```

```python
import functools
import math

import jax
import jax.numpy as jnp
from jax import lax
from jax.experimental import pallas as pl
from jax.experimental.pallas import tpu as pltpu
from jax.sharding import Mesh, PartitionSpec as P


NEG_FILL = -1e30
VMEM_BYTES = 60 * 1024 * 1024
BF = jnp.bfloat16
F32 = jnp.float32
COUNTS = 4


def nt(a, b):
    return lax.dot_general(a, b, (((1,), (1,)), ((), ())), preferred_element_type=F32)


def nn(a, b):
    return lax.dot_general(a, b, (((1,), (0,)), ((), ())), preferred_element_type=F32)


def stack_heads(dst, src):
    rows, width = src.shape
    hd = dst.shape[1]
    for n in range(width // hd):
        dst[n * rows : (n + 1) * rows, :] = src[:, n * hd : (n + 1) * hd]


def fill_window(win, own, other, far_own, far_other, z, zs, cols, rows):
    hd = win.shape[1]

    def at(j, half):
        start = (j + 1) * 2 * rows + half * rows
        return pl.ds(start if isinstance(start, int) else pl.multiple_of(start, rows), rows)

    for half, near, far in ((0, own, far_own), (1, other, far_other)):
        for zz in range(zs):
            win[at(zs + zz, half), :] = near[zz, 0, :rows, :]
            win[at(jnp.where(zz > z, zz, 2 * zs + zz), half), :] = near[zz, 1, :rows, :]
        win[at(z, half), :] = far[:rows, cols]
        win[at(z - 1, half), :] = jnp.zeros((rows, hd), BF)


def out_index(j, z, zs):
    zz = lax.rem(j, zs)
    middle = (j >= zs) & (j < 2 * zs)
    return jnp.where(middle, 2 * zz, jnp.where(j == z, 2 * zs, 2 * zz + 1))


def relative_index(j, z, zs):
    zz = lax.rem(lax.rem(j, zs) + zs - z, zs)
    middle = (j >= zs) & (j < 2 * zs)
    return jnp.where(middle, 2 * zz, jnp.where(j == z, 2 * zs, 2 * zz + 1))


def store_pair(j, value, own, other, z, index):
    rows = own.shape[1]

    @pl.when(j >= z)
    def _():
        own[index(j)] = value[:rows]
        other[index(j)] = value[rows : 2 * rows].astype(other.dtype)

    own[index(j + 1)] = value[2 * rows : 3 * rows]
    other[index(j + 1)] = value[3 * rows :].astype(other.dtype)


def softmax_kernel(
    place_ref,
    q_ref,
    do_ref,
    doc_ref,
    k_own,
    k_other,
    far_own,
    far_other,
    dv_own,
    dv_other,
    p_out,
    info_ref,
    factors,
    q_all,
    do_all,
    k_win,
    p_all,
    raw,
    low,
    state,
    sems,
    *,
    zs,
    scale,
    tile,
    group,
):
    rows, _ = q_ref.shape
    hd = q_all.shape[1]
    total = q_all.shape[0]
    x, z, core = place_ref[0], place_ref[1], place_ref[2]
    base, reach = place_ref[3], place_ref[4]
    here = 2 * zs + z
    unit = scale * math.log2(math.e)

    stack_heads(q_all, q_ref)
    stack_heads(do_all, do_ref)
    fill_window(k_win, k_own, k_other, far_own, far_other, z, zs, slice(0, hd), rows)

    near_ok = (x >= 1).astype(F32)
    far_ok = (x >= 2).astype(F32)
    counts = (
        far_own[rows : rows + COUNTS, :hd].astype(F32)
        + far_other[rows : rows + COUNTS, :hd].astype(F32)
    ) * far_ok
    for zz in range(zs):
        both = k_own[zz, 0, rows : rows + COUNTS, :].astype(F32) + k_other[
            zz, 0, rows : rows + COUNTS, :
        ].astype(F32)
        counts = counts + both * near_ok
        both = k_own[zz, 1, rows : rows + COUNTS, :].astype(F32) + k_other[
            zz, 1, rows : rows + COUNTS, :
        ].astype(F32)
        counts = counts + both * jnp.where(zz > z, far_ok, 1.0)
    doc = doc_ref[...]
    first_row = jnp.zeros((1, rows), F32)
    for d in range(1, COUNTS):
        first_row = jnp.where(doc == d, counts[d : d + 1, :rows], first_row)
    first_row = first_row.astype(jnp.int32) + reach
    lo = (jnp.min(first_row) - base) // (2 * rows)
    edge = jnp.minimum((jnp.max(first_row) - base) // (2 * rows) + 1, here)
    info_ref[0] = lo
    pairs = (here - lo + 2) // 2
    start = here + 1 - 2 * pairs
    inner = jnp.minimum((edge - start + 1) // 2, pairs - 1)
    q_pos = base + (here * 2 + core) * rows + lax.broadcasted_iota(jnp.int32, (1, rows), 1)
    firsts = jnp.concatenate([first_row] * (tile // rows), axis=1)
    lasts = jnp.concatenate([q_pos] * (tile // rows), axis=1)
    key_iota = lax.broadcasted_iota(jnp.int32, (rows, tile), 0)

    state[0:1, :] = jnp.full((1, total), NEG_FILL, F32)
    state[1:2, :] = jnp.zeros((1, total), F32)

    def pair_rows(i):
        return pl.ds(pl.multiple_of((start + 2 * i + 1) * 2 * rows, 2 * rows), 4 * rows)

    def visit(i, masked):
        keys = k_win[pair_rows(i), :]
        for t in range(total // tile):
            cols = slice(t * tile, (t + 1) * tile)
            q_t = q_all[cols, :]
            peak = state[0:1, cols]
            for c in range(4):
                cut = slice(c * rows, (c + 1) * rows)
                s = nt(keys[cut], q_t) * unit
                if masked:
                    chip = start + 2 * i + c // 2
                    key_pos = key_iota + (base + (chip * 2 + (core if c % 2 == 0 else 1 - core)) * rows)
                    s = jnp.where((key_pos >= firsts) & (key_pos <= lasts), s, NEG_FILL)
                peak = jnp.maximum(peak, jnp.max(s, axis=0, keepdims=True))
                raw[cut, cols] = s
            factors[i, 0:1, cols] = peak
        for t in range(total // tile):
            cols = slice(t * tile, (t + 1) * tile)
            old, peak = state[0:1, cols], factors[i, 0:1, cols]
            seen = state[1:2, cols] * jnp.exp2(old - peak)
            for c in range(4):
                cut = slice(c * rows, (c + 1) * rows)
                p = jnp.exp2(raw[cut, cols] - peak)
                p_all[i, cut, cols] = p
                seen = seen + jnp.sum(p, axis=0, keepdims=True)
            state[0:1, cols] = peak
            state[1:2, cols] = seen
        pltpu.make_async_copy(p_all.at[i], p_out.at[i], sems.at[i]).start()

    def plain(i, carry):
        visit(i, False)
        return carry

    def edges(i, carry):
        visit(jnp.where(i < inner, i, pairs - 1), True)
        return carry

    lax.fori_loop(0, inner + 1, edges, 0)
    lax.fori_loop(inner, pairs - 1, plain, 0)
    state[1:2, :] = 1.0 / state[1:2, :]

    def second(i, carry):
        dv = None
        for g in range(total // group):
            for t in range(g * group // tile, (g + 1) * group // tile):
                cols = slice(t * tile, (t + 1) * tile)
                factor = jnp.exp2(factors[i, 0:1, cols] - state[0:1, cols]) * state[1:2, cols]
                factors[i, 0:1, cols] = factor
                for c in range(4):
                    cut = slice(c * rows, (c + 1) * rows)
                    low[cut, cols] = (p_all[i, cut, cols] * factor).astype(BF)
            span = slice(g * group, (g + 1) * group)
            more = nn(low[:, span], do_all[span, :])
            dv = more if dv is None else dv + more
        store_pair(start + 2 * i, dv, dv_own, dv_other, z, lambda j: out_index(j, z, zs))
        return carry

    lax.fori_loop(0, pairs, second, 0)

    def clear(j, carry):
        at = out_index(j, z, zs)
        dv_own[at] = jnp.zeros((rows, hd), F32)
        dv_other[at] = jnp.zeros((rows, hd), BF)
        return carry

    lax.fori_loop(z, lo, clear, 0)

    def finish(i, carry):
        pltpu.make_async_copy(p_all.at[i], p_out.at[i], sems.at[i]).wait()
        return carry

    lax.fori_loop(0, pairs, finish, 0)


def score_kernel(
    place_ref,
    info_ref,
    q_ref,
    do_ref,
    o_ref,
    k_own,
    k_other,
    far_own,
    far_other,
    v_own,
    v_other,
    factors,
    owner_ref,
    p_in,
    packed_ref,
    dk_own,
    dk_other,
    q_all,
    do_all,
    k_win,
    v_win,
    p_all,
    low,
    delta,
    dq_sum,
    sems,
    *,
    zs,
    scale,
    tile,
    group,
    block,
):
    rows, width = q_ref.shape
    hd = q_all.shape[1]
    total = q_all.shape[0]
    z = place_ref[1]
    here = 2 * zs + z
    lo = info_ref[0]

    def copy_in(slot):
        return pltpu.make_async_copy(p_in.at[slot], p_all.at[slot], sems.at[slot])

    pairs = (here - lo + 2) // 2
    start = here + 1 - 2 * pairs

    def begin(i, carry):
        copy_in(i).start()
        return carry

    lax.fori_loop(0, pairs, begin, 0)
    stack_heads(q_all, q_ref)
    stack_heads(do_all, do_ref)
    fill_window(k_win, k_own, k_other, far_own, far_other, z, zs, slice(0, hd), rows)
    fill_window(v_win, v_own, v_other, far_own, far_other, z, zs, slice(hd, 2 * hd), rows)
    for n in range(width // hd):
        cols = slice(n * hd, (n + 1) * hd)
        prod = do_ref[:, cols].astype(F32) * o_ref[:, cols].astype(F32)
        delta[0:1, n * rows : (n + 1) * rows] = jnp.sum(prod.T, axis=0, keepdims=True)
    dq_sum[...] = jnp.zeros_like(dq_sum)

    def clear(j, carry):
        at = relative_index(j, z, zs)
        dk_own[at] = jnp.zeros((rows, hd), F32)
        dk_other[at] = jnp.zeros((rows, hd), BF)
        return carry

    lax.fori_loop(z, lo, clear, 0)

    def visit(i, carry):
        copy_in(i).wait()
        window = pl.ds(pl.multiple_of((start + 2 * i + 1) * 2 * rows, 2 * rows), 4 * rows)
        keys_t = k_win[window, :].T
        values = v_win[window, :]
        dk = None
        for g in range(total // group):
            for t in range(g * group // tile, (g + 1) * group // tile):
                cols = slice(t * tile, (t + 1) * tile)
                do_t = do_all[cols, :]
                for c in range(4):
                    cut = slice(c * rows, (c + 1) * rows)
                    dprob = nt(values[cut], do_t)
                    probs = p_all[i, cut, cols] * factors[i, 0:1, cols]
                    low[cut, cols] = (probs * (dprob - delta[0:1, cols]) * scale).astype(BF)
            span = slice(g * group, (g + 1) * group)
            more = nn(low[:, span], q_all[span, :])
            dk = more if dk is None else dk + more
            dq_sum[:, span] += nn(keys_t, low[:, span])
        store_pair(start + 2 * i, dk, dk_own, dk_other, z, lambda j: relative_index(j, z, zs))
        return carry

    lax.fori_loop(0, pairs, visit, 0)
    half_width = width // 2
    half_heads = half_width // hd
    spots = packed_ref.shape[0]
    row = lax.broadcasted_iota(jnp.int32, (spots, rows), 0)
    token = lax.broadcasted_iota(jnp.int32, (spots, rows), 1)
    slots = owner_ref.shape[1]
    spread = lax.broadcasted_iota(jnp.int32, (slots, rows), 1) // block
    spread = spread == lax.broadcasted_iota(jnp.int32, (slots, rows), 0)
    owners = jnp.broadcast_to(owner_ref[...].astype(F32).astype(BF), (8, slots))
    owners = nn(owners, spread.astype(F32).astype(BF))[0:1]
    goes = ((row // (2 * block)).astype(F32) == owners) & (row % block == token % block)
    packed = jnp.zeros((spots, half_width), F32)
    for h in range(2):
        here_half = goes & (row // block % 2 == h)
        turned = [
            dq_sum[:, n * rows : (n + 1) * rows].T.astype(BF)
            for n in range(h * half_heads, (h + 1) * half_heads)
        ]
        packed = packed + nn(here_half.astype(F32).astype(BF), jnp.concatenate(turned, axis=1))
    packed_ref[...] = packed.astype(BF)


def swap(value):
    return lax.ppermute(value, "core", [(0, 1), (1, 0)])


def first_payload_kernel(keys_ref, values_ref, doc_ref, owner_ref, out_ref, notes, *, xs):
    part, groups, hd = keys_ref.shape
    extra, width = notes.shape
    per_device = owner_ref.shape[1]
    row = lax.broadcasted_iota(jnp.int32, (extra, doc_ref.shape[1]), 0)
    earlier = jnp.sum((doc_ref[...] < row).astype(F32), axis=1, keepdims=True)
    notes[...] = jnp.broadcast_to(earlier, (extra, width))
    notes[COUNTS:, :per_device] = jnp.broadcast_to(
        owner_ref[...].astype(F32), (extra - COUNTS, per_device)
    )
    low = notes[...].astype(BF)
    for g in range(groups):
        k, v = keys_ref[:, g, :], values_ref[:, g, :]
        for at in range(g * xs, (g + 1) * xs):
            out_ref[at, :part, :hd] = k
            out_ref[at, :part, hd:] = v
            out_ref[at, part:, :] = low


def pick_kernel(place_ref, k_own, k_other, pick_ref, *, block, per_device, xs):
    zs, _, tall, hd = k_own.shape
    extra = COUNTS + xs
    first = tall - extra
    rows, spots = pick_ref.shape[1:]
    core, me = place_ref[2], place_ref[5]
    slot = lax.broadcasted_iota(jnp.int32, (rows, hd), 0) // block
    to_rows = (slot == lax.broadcasted_iota(jnp.int32, (rows, hd), 1)).astype(F32).astype(BF)
    held = lax.broadcasted_iota(jnp.int32, (zs * extra, hd), 0) % extra >= COUNTS
    held = held & (lax.broadcasted_iota(jnp.int32, (zs * extra, hd), 1) < per_device)
    line = lax.broadcasted_iota(jnp.int32, (zs * extra, spots), 0)
    peer = lax.broadcasted_iota(jnp.int32, (zs * extra, spots), 1) // (2 * block)
    pick = jnp.zeros((rows, spots), F32)
    for notes, c in ((k_own, core), (k_other, 1 - core)):
        owners = jnp.concatenate([notes[zz, 0, first:, :].astype(F32) for zz in range(zs)], axis=0)
        hit = (held & (owners == me.astype(F32))).astype(F32).astype(BF)
        source = ((line % extra - COUNTS) * zs + line // extra) * 2 + c
        to_spots = ((source == peer) & (line % extra >= COUNTS)).astype(F32).astype(BF)
        pick = pick + nn(nt(to_rows, hit).astype(BF), to_spots)
    row = lax.broadcasted_iota(jnp.int32, (rows, spots), 0)
    spot = lax.broadcasted_iota(jnp.int32, (rows, spots), 1)
    same = spot % block == row % block
    for h in range(2):
        pick_ref[h] = jnp.where(same & (spot // block % 2 == h), pick, 0.0).astype(BF)


def placement_kernel(pick_ref, arrived_ref, out_ref):
    half_width = arrived_ref.shape[1]
    for h in range(2):
        out_ref[:, h * half_width : (h + 1) * half_width] = nn(
            pick_ref[h], arrived_ref[...]
        ).astype(BF)


def along_x(parts, xs):
    mine, near, far = parts
    from_next = lax.ppermute(near, "x", [(i, i - 1) for i in range(1, xs)])
    from_last = lax.ppermute(far, "x", [(i, i - 2) for i in range(2, xs)])
    return (mine + from_next + from_last).astype(BF)


def reduce_at_once(own, other, zs):
    rows, hd = own.shape[1:]
    swapped = swap(other)
    sent = (own[: 2 * zs] + swapped[: 2 * zs].astype(F32)).astype(BF).reshape(zs, 2, rows, hd)
    came = lax.all_to_all(sent, "z", split_axis=0, concat_axis=0, tiled=True)
    return came, own[2 * zs] + swapped[2 * zs].astype(F32)


def sum_arrived(came, far, zs, z):
    came = came.astype(F32)
    later = (jnp.arange(zs) >= z)[:, None, None]
    mine = jnp.sum(jnp.where(later, came[:, 1], 0.0), axis=0)
    near = jnp.sum(came[:, 0], axis=0)
    far = jnp.sum(jnp.where(later, 0.0, came[:, 1]), axis=0) + far
    return mine, near, far


def reduce_by_shifts(own, other, zs, z):
    swapped = swap(other)

    def both(at):
        return own[at] + swapped[at].astype(F32)

    came = []
    for k in range(1, zs):
        sent = both(slice(2 * k, 2 * k + 2)).astype(BF)
        came.append(lax.ppermute(sent, "z", [(i, (i + k) % zs) for i in range(zs)]))
    mine, near, far = both(1), both(0), both(2 * zs)
    for k, got in enumerate(came, 1):
        near = near + got[0].astype(F32)
        mine = mine + jnp.where(z < k, got[1].astype(F32), 0.0)
        far = far + jnp.where(z < k, 0.0, got[1].astype(F32))
    return mine, near, far


def program(queries, keys, values, outputs, grad_out, doc_ids, owner):
    hd = keys.shape[2]
    scale = hd**-0.5
    rows, _, width = queries.shape
    total = rows * (width // hd)
    tile = min(256, total)
    group = min(1024, total)
    xs, zs = lax.axis_size("x"), lax.axis_size("z")
    x, z, core = lax.axis_index("x"), lax.axis_index("z"), lax.axis_index("core")
    peers = xs * zs * 2
    per_device = owner.shape[0]
    block_len = rows // per_device
    part = keys.shape[0]
    chips = 2 * zs + 1
    steps = zs + 1

    extra = COUNTS + xs
    vmem = pl.BlockSpec(memory_space=pltpu.VMEM)
    smem = pl.BlockSpec(memory_space=pltpu.SMEM)
    anywhere = pl.BlockSpec(memory_space=pl.ANY)
    mixed = pl.pallas_call(
        functools.partial(first_payload_kernel, xs=xs),
        in_specs=[vmem] * 4,
        out_specs=vmem,
        out_shape=jax.ShapeDtypeStruct((4 * xs, part + extra, 2 * hd), BF),
        scratch_shapes=[pltpu.VMEM((extra, 2 * hd), F32)],
        name="first_payload",
    )(keys, values, doc_ids[None], owner[None])
    mixed = lax.all_to_all(
        mixed,
        ("dp", "head", "x"),
        split_axis=0,
        concat_axis=0,
        tiled=True,
    ).reshape(2, 2, xs, part + extra, 2 * hd)

    def piece(back):
        got = lax.dynamic_index_in_dim(mixed, lax.rem(x - back + xs, xs), 2, keepdims=False)
        tokens = jnp.transpose(got[:, :, :part], (1, 0, 2, 3)).reshape(rows, 2 * hd)
        return jnp.concatenate([tokens, got[0, 0, part:]], axis=0)

    last, near, far = piece(0), piece(1), piece(2)
    far_other = swap(far)

    def along_z(a, b, c):
        ahead = (jnp.arange(zs) >= z)[:, None, None]
        chosen = jnp.where(ahead, a[None], c[None])
        pair = jnp.stack([jnp.broadcast_to(b[None], chosen.shape), chosen], axis=1)
        return lax.all_to_all(pair, "z", split_axis=0, concat_axis=0, tiled=True)

    held = mixed[0, 0, :, part + COUNTS, :hd]
    near_keys = jnp.concatenate([near[: rows + COUNTS, :hd], held], axis=0)
    k_own = along_z(last[:, :hd], near_keys, far[:, :hd])
    k_other = swap(k_own)
    v_own = along_z(last[:rows, hd:], near[:rows, hd:], far[:rows, hd:])

    base = (x - 2) * (zs * 2 * rows)
    me = (x * zs + z) * 2 + core
    place = jnp.stack([x, z, core, base, jnp.maximum(base + z * 2 * rows, 0), me]).astype(jnp.int32)
    q = queries.reshape(rows, width)
    do = grad_out.reshape(rows, width)
    o = outputs.reshape(rows, width)
    own_shape = jax.ShapeDtypeStruct((chips, rows, hd), F32)
    other_shape = jax.ShapeDtypeStruct((chips, rows, hd), BF)
    params = pltpu.CompilerParams(vmem_limit_bytes=VMEM_BYTES)
    small = pltpu.CompilerParams(vmem_limit_bytes=8 * 1024 * 1024)
    dv_own, dv_other, probs, info, factors = pl.pallas_call(
        functools.partial(softmax_kernel, zs=zs, scale=scale, tile=tile, group=group),
        in_specs=[smem] + [vmem] * 7,
        out_specs=[vmem, vmem, anywhere, smem, vmem],
        out_shape=[
            own_shape,
            other_shape,
            jax.ShapeDtypeStruct((steps, 4 * rows, total), F32),
            jax.ShapeDtypeStruct((1,), jnp.int32),
            jax.ShapeDtypeStruct((steps, 8, total), F32),
        ],
        scratch_shapes=[
            pltpu.VMEM((total, hd), BF),
            pltpu.VMEM((total, hd), BF),
            pltpu.VMEM(((3 * zs + 1) * 2 * rows, hd), BF),
            pltpu.VMEM((steps, 4 * rows, total), F32),
            pltpu.VMEM((4 * rows, total), F32),
            pltpu.VMEM((4 * rows, total), BF),
            pltpu.VMEM((8, total), F32),
            pltpu.SemaphoreType.DMA((steps,)),
        ],
        compiler_params=params,
        cost_estimate=pl.CostEstimate(
            flops=12_000_000_000, bytes_accessed=20_000_000, transcendentals=4_000_000
        ),
        name="softmax_and_value_gradient",
    )(
        place,
        q,
        do,
        doc_ids.reshape(1, rows),
        k_own,
        k_other,
        far,
        far_other,
    )
    v_other = swap(v_own)
    came_v, far_v = reduce_at_once(dv_own, dv_other, zs)
    packed, dk_own, dk_other = pl.pallas_call(
        functools.partial(
            score_kernel, zs=zs, scale=scale, tile=tile, group=group, block=block_len
        ),
        in_specs=[smem, smem] + [vmem] * 11 + [anywhere],
        out_specs=[vmem] * 3,
        out_shape=[
            jax.ShapeDtypeStruct((peers * 2 * block_len, width // 2), BF),
            own_shape,
            other_shape,
        ],
        scratch_shapes=[
            pltpu.VMEM((total, hd), BF),
            pltpu.VMEM((total, hd), BF),
            pltpu.VMEM(((3 * zs + 1) * 2 * rows, hd), BF),
            pltpu.VMEM(((3 * zs + 1) * 2 * rows, hd), BF),
            pltpu.VMEM((steps, 4 * rows, total), F32),
            pltpu.VMEM((4 * rows, total), BF),
            pltpu.VMEM((8, total), F32),
            pltpu.VMEM((hd, total), F32),
            pltpu.SemaphoreType.DMA((steps,)),
        ],
        compiler_params=params,
        cost_estimate=pl.CostEstimate(
            flops=12_000_000_000, bytes_accessed=20_000_000, transcendentals=0
        ),
        name="score_gradient",
    )(
        place,
        info,
        q,
        do,
        o,
        k_own,
        k_other,
        far,
        far_other,
        v_own,
        v_other,
        factors,
        owner[None],
        probs,
    )
    parts_k = reduce_by_shifts(dk_own, dk_other, zs, z)
    parts_v = sum_arrived(came_v, far_v, zs, z)
    grads = along_x([jnp.concatenate(pair, axis=1) for pair in zip(parts_k, parts_v)], xs)
    grad_k, grad_v = grads[:, None, :hd], grads[:, None, hd:]

    pick = pl.pallas_call(
        functools.partial(pick_kernel, block=block_len, per_device=per_device, xs=xs),
        in_specs=[smem, vmem, vmem],
        out_specs=vmem,
        out_shape=jax.ShapeDtypeStruct((2, rows, peers * 2 * block_len), BF),
        cost_estimate=pl.CostEstimate(flops=100_000_000, bytes_accessed=1_000_000, transcendentals=0),
        compiler_params=small,
        name="placement_choice",
    )(place, k_own, k_other)
    arrived = lax.all_to_all(
        packed.reshape(peers, 2 * block_len, width // 2),
        ("x", "z", "core"),
        split_axis=0,
        concat_axis=0,
        tiled=True,
    )
    placed = pl.pallas_call(
        placement_kernel,
        in_specs=[vmem, vmem],
        out_specs=vmem,
        out_shape=jax.ShapeDtypeStruct((rows, width), BF),
        compiler_params=small,
        name="query_gradient_placement",
    )(pick, arrived.reshape(packed.shape))
    return (placed.reshape(rows, 1, width), grad_k, grad_v)


def solution(mesh):
    sizes = mesh.shape
    dp, ctx, head = sizes["dp"], sizes["ctx"], sizes["head"]
    xs = 4
    fine = Mesh(
        mesh.devices.reshape(dp, xs, ctx // (2 * xs), 2, head), ("dp", "x", "z", "core", "head")
    )
    ctx_axes = ("x", "z", "core")
    heads = P(ctx_axes, ("dp", "head"), None)
    tokens = P(ctx_axes + ("head", "dp"), None, None)
    return jax.shard_map(
        program,
        mesh=fine,
        in_specs=(heads, tokens, tokens, heads, heads, P(ctx_axes), P(ctx_axes)),
        out_specs=(heads, heads, heads),
        check_vma=False,
    )
```
